32 devices in a mesh: angle: 8 (over z, y), tile: 2 (over x), half: 2 (over core).
Axes of the slice: x: 2, y: 2, z: 4, core: 2. Of those that a mesh axis runs over, the one named last changes fastest.
Arguments:
- projection: float32 [16, 2, 64, 256], P(('angle', 'half'), None, 'tile'), may hold values from -6 to 6
- multiplier: float32 [16, 2, 64, 256], P(('angle', 'half'), None, 'tile'), may hold values from -3 to 3
- reprojection: float32 [16, 64, 256], P(('angle', 'half'), 'tile'), may hold values from -6 to 6
- intensity: bfloat16 [16, 64, 64, 128], P(('angle', 'half'), 'tile'), may hold values from 0 to 4
- row_start: int32 [16, 64], P(('angle', 'half'), 'tile'), may hold values from -32 to 0
- column_start: int32 [16, 64], P(('angle', 'half'), 'tile'), may hold values from 0 to 128
- probe_field: float32 [2, 64, 128], replicated, may hold values from -6 to 6
- probe_mask: int32 [64, 128], replicated, may hold values 0 or 1
- weights: bfloat16 [16, 2, 4, 128, 512], P('angle'), may hold values from -0.125 to 0.125
- ray_blocks: int32 [16, 2, 4], P('angle'), may hold values from 0 to 127, as said below
- ray_counts: int32 [16, 2], P('angle'), may hold values from 1 to 4, as said below
- volume: float32 [128, 64, 512], P('angle', ('tile', 'half')), may hold values from -6 to 6
Outputs:
- updated_projection: float32 [16, 2, 64, 256], P(('angle', 'half'), None, 'tile')
- volume_new: float32 [128, 64, 512], P('angle', ('tile', 'half'))
- multiplier_new: float32 [16, 2, 64, 256], P('angle', None, ('tile', 'half'))
The draws below stay inside these ranges and needn't reach their ends.
Inputs may be any that keep to these rules, and one draw needn't show every extreme that they name: A ray block uses its first ray_counts weight tiles; some ray block uses all 4. `ray_blocks`: slots at or past a ray block's count are not used. Split the angles into aligned groups of 2 and the pixel blocks into aligned groups of 16: the 16 slots of one angle group name blocks of one block group at most 2 times, and exactly 2 times for some block group.
All inputs are finite; a program needn't handle non-finite values.
Results may differ from the reference program's by a relative error of at most 0.008.
Values may be sent and summed in bfloat16 or wider, within the bound.
A program may use at most 64 MiB of HBM per device.

```python
import jax
import jax.numpy as jnp
from jax import lax

PR = 64
PC = 128
NW = 256
PIX = 512
RB = 128
CMAX = 4
BAND = 32
P_DEV = 32
HALO = 32
ANGLES = 16
ANG_T = 2
SLICES = 64
NRB = 2
NPB = 128
CAP = 2
PATCHES = 64


def draw_ray_counts(key, part):
    first, second, third = jax.random.split(key, 3)
    base = jax.random.randint(first, (ANGLES * NRB,), 1, CMAX + 1)
    heavy = jax.random.randint(second, (ANGLES * NRB,), 0, 3)
    counts = jnp.where(heavy == 0, CMAX, base)
    position = jax.random.randint(third, (), 0, ANGLES * NRB)
    counts = counts.at[position].set(CMAX)
    return counts.reshape(ANGLES, NRB).astype(jnp.int32)


def draw_ray_blocks(key, part):
    groups = ANGLES // ANG_T
    owned = NPB // groups
    slot_count = ANG_T * NRB * CMAX
    base = jax.random.fold_in(key, 7)
    group_keys = jax.random.split(base, groups)

    def one_group(group_key):
        first, second, third, fourth = jax.random.split(group_key, 4)
        leader = jax.random.randint(first, (), 0, groups)
        others = (leader + 1 + jnp.arange(groups - 1, dtype=jnp.int32)) % groups
        others = jax.random.permutation(second, jnp.repeat(others, CAP))
        owners = jnp.concatenate([jnp.full((CAP,), leader, jnp.int32), others])[:slot_count]
        owners = jax.random.permutation(third, owners)
        inside = jax.random.randint(fourth, (slot_count,), 0, owned)
        return (owners * owned + inside).astype(jnp.int32)
    blocks = jax.vmap(one_group)(group_keys)
    return blocks.reshape(ANGLES, NRB, CMAX).astype(jnp.int32)


def set_ends(drawn, key, smallest, top_value):
    place = [jax.random.randint(jax.random.fold_in(key, axis), (), 0, length) for axis, length in enumerate(drawn.shape)]
    main_axis = drawn.shape.index(max(drawn.shape))
    neighbour = place[:main_axis] + [(place[main_axis] + 1) % drawn.shape[main_axis]] + place[main_axis + 1:]
    return drawn.at[tuple(place)].set(smallest).at[tuple(neighbour)].set(top_value)


def block_scale(stream_key, shape, cuts, low, high):
    def one(dim, blocks):
        draws = jax.random.uniform(jax.random.fold_in(jax.random.fold_in(stream_key, 6), dim), (blocks,), jnp.float32, low / len(cuts), high / len(cuts))
        return jnp.repeat(jnp.exp(draws), shape[dim] // blocks).reshape((-1,) + (1,) * (len(shape) - dim - 1))

    factor_of = one(*cuts[0])
    for cut in cuts[1:]:
        factor_of = factor_of * one(*cut)
    return factor_of


def centred(rng, extent, scale, most, cuts=(), kind=jnp.bfloat16):
    entries = jax.random.normal(rng, extent, jnp.float32) * scale
    if len(cuts) > 0:
        entries = block_scale(rng, extent, cuts, -0.22, 0.18) * entries
    return jnp.clip(entries, min=-most, max=most).astype(kind)


def setup_inputs(seed: int = 0) -> dict:
    streams_of = jax.random.split(jax.random.key(seed), 13)
    return {
        "projection": centred(streams_of[0], (ANGLES, 2, SLICES, NW), 1.0, 6.0, ((0, 16), (2, 2)), jnp.float32),
        "multiplier": centred(streams_of[1], (ANGLES, 2, SLICES, NW), 0.5, 3.0, ((0, 16), (2, 2)), jnp.float32),
        "reprojection": centred(streams_of[2], (ANGLES, SLICES, NW), 1.0, 6.0, ((0, 16), (1, 2)), jnp.float32),
        "intensity": jnp.clip(4.0 * jax.random.uniform(streams_of[3], (ANGLES, PATCHES, PR, PC), jnp.float32) ** block_scale(streams_of[3], (ANGLES, PATCHES, PR, PC), ((0, 16), (1, 2)), -0.2, 0.2), 0.0, 4.0).astype(jnp.bfloat16),
        "row_start": set_ends(jax.random.randint(streams_of[4], (ANGLES, PATCHES), 0 - HALO, BAND + HALO - PR + 1), jax.random.fold_in(streams_of[4], 1), 0 - HALO, BAND + HALO - PR).astype(jnp.int32),
        "column_start": set_ends(jax.random.randint(streams_of[5], (ANGLES, PATCHES), 0, NW - PC + 1), jax.random.fold_in(streams_of[5], 1), 0, NW - PC).astype(jnp.int32),
        "probe_field": centred(streams_of[6], (2, PR, PC), 1.0, 6.0, (), jnp.float32),
        "probe_mask": set_ends((jax.random.randint(streams_of[7], (PR, PC), 0, 4) < 3).astype(jnp.int32), jax.random.fold_in(streams_of[7], 1), 0, 1),
        "weights": centred(streams_of[8], (ANGLES, NRB, CMAX, RB, PIX), (CMAX * PIX) ** -0.5, 0.125, ((0, 8),)),
        "ray_blocks": draw_ray_blocks(jax.random.fold_in(streams_of[12], 71), 0),
        "ray_counts": draw_ray_counts(jax.random.fold_in(streams_of[12], 71), 0),
        "volume": centred(streams_of[11], (NPB, SLICES, PIX), 1.0, 6.0, ((0, 8), (1, 4)), jnp.float32),
    }


penalty = 0.5
descent = 0.25
volume_step = 1.0
damping = 0.1
highest = lax.Precision.HIGHEST

def to_half(values):
    return lax.optimization_barrier(values.astype(jnp.bfloat16)).astype(jnp.float32)

def ptycho_angle(inputs, masked_probe):
    object_band, mult_band, prior_band, measured, rows_in, columns_in = inputs
    padded = jnp.pad(object_band, ((0, 0), (HALO, HALO), (0, 0)))
    offsets = jnp.arange(PATCHES, dtype=jnp.int32) // P_DEV * BAND + rows_in.astype(jnp.int32) + HALO
    zero_index = jnp.zeros((), jnp.int32)

    def cutout(first_row, first_column):
        return lax.dynamic_slice(padded, (zero_index, first_row, first_column), (2, PR, PC))
    pieces = jax.vmap(cutout)(offsets, columns_in.astype(jnp.int32))
    wave_real = masked_probe[0] * pieces[:, 0] - masked_probe[1] * pieces[:, 1]
    wave_imag = masked_probe[0] * pieces[:, 1] + masked_probe[1] * pieces[:, 0]
    far = jnp.fft.fft2(lax.complex(wave_real, wave_imag), norm='ortho')
    far_real = jnp.real(far)
    far_imag = jnp.imag(far)
    factor = 1.0 - jnp.sqrt(measured.astype(jnp.float32)) / jnp.sqrt(far_real * far_real + far_imag * far_imag + 1.0)
    back = jnp.fft.ifft2(lax.complex(far_real * factor, far_imag * factor), norm='ortho')
    back_real = jnp.real(back)
    back_imag = jnp.imag(back)
    grad_real = masked_probe[0] * back_real + masked_probe[1] * back_imag
    grad_imag = masked_probe[0] * back_imag - masked_probe[1] * back_real
    patch_grads = jnp.stack([grad_real, grad_imag], axis=1)

    def accumulate(total, item):
        values, first_row, first_column = item
        window = lax.dynamic_slice(total, (zero_index, first_row, first_column), (2, PR, PC))
        return (lax.dynamic_update_slice(total, window + values, (zero_index, first_row, first_column)), None)
    total, unused = lax.scan(accumulate, jnp.zeros_like(padded), (patch_grads, offsets, columns_in.astype(jnp.int32)))
    gradient = total[:, HALO:HALO + SLICES]
    holder = jnp.stack([jnp.ones_like(prior_band), prior_band], axis=0)
    return object_band - descent * (gradient + penalty * (object_band - holder) + mult_band)

def live_slots(block_count):
    return (jnp.arange(CMAX, dtype=jnp.int32)[None, :] < block_count[:, None]).astype(jnp.float32)

def project(field, weights, ray_blocks, ray_counts):

    def one_angle(inputs):
        tile_weights, block_index, block_count = inputs
        masked = tile_weights.astype(jnp.float32) * live_slots(block_count)[:, :, None, None]
        picked = field[block_index]
        result = jnp.einsum('kcrp,kcsp->skr', masked, picked, precision=highest)
        return result.reshape(SLICES, NW)
    return lax.map(one_angle, (weights, ray_blocks, ray_counts))

def reference(projection, multiplier, reprojection, intensity, row_start, column_start, probe_field, probe_mask, weights, ray_blocks, ray_counts, volume):
    masked_probe = probe_field * probe_mask.astype(jnp.float32)[None]
    updated = lax.map(lambda inputs: ptycho_angle(inputs, masked_probe), (projection, multiplier, reprojection, intensity, row_start, column_start))
    target = updated[:, 1] + multiplier[:, 1] / penalty
    sinogram = project(to_half(volume), weights, ray_blocks, ray_counts)
    residual = to_half(sinogram - target)

    def spread_angle(total, inputs):
        tile_weights, block_index, block_count, residual_angle = inputs
        masked = tile_weights.astype(jnp.float32) * live_slots(block_count)[:, :, None, None]
        spread = jnp.einsum('kcrp,skr->kcsp', masked, residual_angle.reshape(SLICES, NRB, RB), precision=highest)
        return (total.at[block_index.reshape(-1)].add(spread.reshape(NRB * CMAX, SLICES, PIX)), None)
    block_gradient, unused = lax.scan(spread_angle, jnp.zeros((NPB, SLICES, PIX), jnp.float32), (weights, ray_blocks, ray_counts, residual))
    volume_new = volume - volume_step * (block_gradient + damping * volume)
    fresh = project(to_half(volume_new), weights, ray_blocks, ray_counts)
    fresh_holder = jnp.stack([jnp.ones_like(fresh), fresh], axis=1)
    multiplier_new = multiplier + penalty * (updated - fresh_holder)
    return (updated, volume_new, multiplier_new)
```

```python
import functools

import jax
import jax.numpy as jnp
import numpy as np
from jax import lax
from jax.experimental import pallas as pl
from jax.experimental.pallas import tpu as pltpu
from jax.sharding import PartitionSpec as P

PR = 64
PC = 128
NW = 256
PIX = 512
RB = 128
CMAX = 4
HALO = 32
NRB = 2


penalty = 0.5
descent = 0.25
volume_step = 1.0
damping = 0.1


def dft_blocks(sign):
    def table(length):
        counter = np.arange(length)
        phase = (counter[:, None] * counter[None, :] % length) * (2.0 * np.pi / length)
        return np.cos(phase) / np.sqrt(length), sign * np.sin(phase) / np.sqrt(length)

    row_cos, row_sin = table(PR)
    col_cos, col_sin = table(PC)
    left = np.block([[row_cos, -row_sin], [row_sin, row_cos]])
    right = np.block([[col_cos, col_sin], [-col_sin, col_cos]])
    return left.astype(np.float32), right.astype(np.float32)


def split_table(matrix):
    coarse = matrix.astype(jnp.bfloat16)
    rest = (matrix - coarse.astype(np.float32)).astype(jnp.bfloat16)
    return jnp.asarray(np.concatenate([coarse, rest], axis=1))


MESH = pl.DeviceIdType.MESH
CHUNK = 16
ROWS = 8
LANES = 128


def orders(groups):
    rising = list(range(1, groups))
    paired = []
    for d in range(1, groups // 2 + 1):
        paired += [groups - d] if 2 * d == groups else [groups - d, d]
    if groups % 2:
        paired = rising
    return rising, paired


def step_kernel(
    groups, tiles, capacity,
    mine_hbm, counts_hbm, rows_hbm, cols_hbm, proj_hbm, mult_hbm, prior_hbm, field_hbm, mask_hbm,
    left_f_hbm, right_f_hbm, left_b_hbm, right_b_hbm, measured_hbm, vol_hbm, weight_hbm,
    updated_ref, new_vol_ref, new_mult_ref,
    mine_ref, counts_ref, rows_ref, cols_ref, proj_ref, mult_ref, prior_ref, field_ref, mask_ref,
    left_f_ref, right_f_ref, left_b_ref, right_b_ref, measured_ref, vol_ref, weight_ref,
    all_smem, place_ref, inside_ref, slot_ref, used_ref, live_ref,
    ids_ref, all_ref, edge_ref, before_ref, after_ref,
    ext_ref, acc_ref, wave_ref, stage_ref,
    base_ref, grad_ref, both_base_ref, both_mult_ref, both_grad_ref,
    rim_ref, rim_here_ref, rim_away_ref,
    vol_half_ref, merge_ref, residual_ref,
    send_a, send_b, send_c, recv_a, recv_b, recv_c,
    send_sem, recv_sem, near_send, near_recv, local_sem,
):
    g = lax.axis_index("angle")
    t = lax.axis_index("tile")
    h = lax.axis_index("half")
    band = proj_ref.shape[2]
    part = band // 2
    places = groups * capacity
    own_blocks = vol_ref.shape[0]
    angles, blocks, per_block = mine_ref.shape
    slots = angles * blocks * per_block
    pairs = slots // per_block
    has_up = t > 0
    has_down = t < tiles - 1
    half = jnp.bfloat16
    sends = (send_a, send_b, send_c)
    recvs = (recv_a, recv_b, recv_c)
    lanes = [slice(0, PC), slice(PC, NW)]
    rising, paired = orders(groups)

    def where_of(slot):
        pair, c = divmod(slot, per_block)
        angle, block = divmod(pair, blocks)
        return angle, block, c

    barrier = pltpu.get_barrier_semaphore()

    def greet(where):
        pl.semaphore_signal(barrier, inc=1, device_id=where, device_id_type=MESH)

    for d in rising:
        greet({"angle": lax.rem(g + d, groups)})
    greet({"half": 1 - h})

    @pl.when(has_up)
    def _():
        greet({"tile": t - 1})
        greet({"tile": t - 1, "half": 1 - h})

    @pl.when(has_down)
    def _():
        greet({"tile": t + 1})
        greet({"tile": t + 1, "half": 1 - h})

    sources = (
        mine_hbm, counts_hbm, rows_hbm, cols_hbm, proj_hbm, mult_hbm, prior_hbm, field_hbm, mask_hbm,
        left_f_hbm, right_f_hbm, left_b_hbm, right_b_hbm, measured_hbm, vol_hbm, weight_hbm,
    )
    targets = (
        mine_ref, counts_ref, rows_ref, cols_ref, proj_ref, mult_ref, prior_ref, field_ref, mask_ref,
        left_f_ref, right_f_ref, left_b_ref, right_b_ref, measured_ref, vol_ref, weight_ref,
    )
    loads = [
        pltpu.make_async_copy(source, target, local_sem.at[i])
        for i, (source, target) in enumerate(zip(sources, targets))
    ]
    for load in loads:
        load.start()

    @pl.when(jnp.logical_not(has_up))
    def _():
        before_ref[...] = jnp.zeros_like(before_ref)
        rim_here_ref[0] = jnp.zeros(rim_here_ref.shape[1:], half)
        rim_away_ref[0] = jnp.zeros(rim_away_ref.shape[1:], half)

    @pl.when(jnp.logical_not(has_down))
    def _():
        after_ref[...] = jnp.zeros_like(after_ref)
        rim_here_ref[1] = jnp.zeros(rim_here_ref.shape[1:], half)
        rim_away_ref[1] = jnp.zeros(rim_away_ref.shape[1:], half)

    acc_ref[...] = jnp.zeros_like(acc_ref)
    stage_ref[...] = jnp.zeros_like(stage_ref)
    ids_ref[...] = jnp.zeros_like(ids_ref)

    for load in loads[:2]:
        load.wait()
    blocks_of = [mine_ref[where_of(s)] for s in range(slots)]
    owners = [lax.div(b, own_blocks) for b in blocks_of]
    for s in range(slots):
        rank = jnp.int32(0)
        for earlier in range(s):
            rank = rank + jnp.where(owners[earlier] == owners[s], 1, 0)
        place_ref[s] = owners[s] * capacity + rank
        inside_ref[s] = lax.rem(blocks_of[s], own_blocks)
        angle, block, c = where_of(s)
        live_ref[s] = jnp.where(c < counts_ref[angle, block], 1.0, 0.0)

    def slot_of(n, carry):
        slot = jnp.int32(0)
        used = jnp.float32(0.0)
        for s in range(slots):
            hit = place_ref[s] == n
            slot = jnp.where(hit, s, slot)
            used = jnp.where(hit, live_ref[s], used)
        slot_ref[n] = slot
        used_ref[n] = used
        return carry

    lax.fori_loop(0, places, slot_of, 0)
    for n in range(places):
        q, r = divmod(n, capacity)
        ids_ref[q, r : r + 1, :] = jnp.full((1, LANES), inside_ref[slot_ref[n]], jnp.int32)

    away = pl.ds(pl.multiple_of((1 - h) * part, part), part)
    here = pl.ds(pl.multiple_of(h * part, part), part)
    for load in loads[4:9]:
        load.wait()
    edge_ref[...] = proj_ref[0].astype(half)
    for channel in range(2):
        old = proj_ref[0, channel]
        held = 1.0 if channel == 0 else prior_ref[0]
        base_ref[channel] = old - descent * (penalty * (old - held) + mult_ref[0, channel])
    for side in range(2):
        ext_ref[:, side, HALO : HALO + band] = proj_ref[0, :, :, lanes[side]]
    mask = mask_ref[...].astype(jnp.float32)
    wave_ref[0] = field_ref[0] * mask
    wave_ref[1] = field_ref[1] * mask
    both_base_ref[h] = base_ref[:, here, :]
    both_mult_ref[h] = mult_ref[0, :, here, :]
    loads[14].wait()
    vol_half_ref[...] = vol_ref[...].astype(half)

    pl.semaphore_wait(
        barrier, groups + 2 * has_up.astype(jnp.int32) + 2 * has_down.astype(jnp.int32)
    )

    def angle_copy(phase, d, source, target):
        return pltpu.make_async_remote_copy(
            src_ref=source,
            dst_ref=target,
            send_sem=send_sem.at[phase, d],
            recv_sem=recv_sem.at[phase, d],
            device_id={"angle": lax.rem(g + d, groups)},
            device_id_type=MESH,
        )

    def near(index, source, target, where):
        return pltpu.make_async_remote_copy(
            src_ref=source,
            dst_ref=target,
            send_sem=near_send.at[index],
            recv_sem=near_recv.at[index],
            device_id=where,
            device_id_type=MESH,
        )

    below = jnp.minimum(t + 1, tiles - 1)
    upper = jnp.maximum(t - 1, 0)

    def when_sent(way, act):
        pl.when(has_down if way == 0 else has_up)(act)

    def when_received(way, act):
        pl.when(has_up if way == 0 else has_down)(act)

    id_copies = [
        angle_copy(3, d, ids_ref.at[lax.rem(g + d, groups)], all_ref.at[g]) for d in rising
    ]
    for copy in id_copies:
        copy.start()
    halo = [
        near(0, edge_ref, before_ref, {"tile": below}),
        near(1, edge_ref, after_ref, {"tile": upper}),
    ]
    for way in range(2):
        when_sent(way, halo[way].start)
    base_copy = near(2, base_ref.at[:, away, :], both_base_ref.at[h], {"half": 1 - h})
    mult_copy = near(3, mult_ref.at[0, :, away, :], both_mult_ref.at[h], {"half": 1 - h})
    base_copy.start()
    mult_copy.start()
    all_ref[g] = ids_ref[g]
    for load in loads[2:4] + loads[9:14]:
        load.wait()
    for way in range(2):
        when_received(way, halo[way].wait_recv)
    for side in range(2):
        ext_ref[:, side, :HALO] = before_ref[:, :, lanes[side]].astype(jnp.float32)
        ext_ref[:, side, HALO + band :] = after_ref[:, :, lanes[side]].astype(jnp.float32)

    lane = lax.broadcasted_iota(jnp.int32, (PR, PC), 1)
    ext_rows = band + 2 * HALO
    wide_lane = lax.broadcasted_iota(jnp.int32, (ext_rows, PC), 1)

    def dot(a, b):
        return jnp.dot(a, b, preferred_element_type=jnp.float32)

    def step(chunk, carry):
        waves = []
        spots = []
        for j in range(CHUNK):
            p = chunk * CHUNK + j
            row = rows_ref[0, p] + HALO
            col = cols_ref[0, p]
            spots.append((row, col))
            back_shift = lax.rem(NW - col, PC)

            def window(channel):
                near = pltpu.roll(ext_ref[channel, 0, pl.ds(row, PR), :], back_shift, 1)
                next_ = pltpu.roll(ext_ref[channel, 1, pl.ds(row, PR), :], back_shift, 1)
                return jnp.where(lane + col < PC, near, next_)

            o_re = window(0)
            o_im = window(1)
            p_re, p_im = wave_ref[0], wave_ref[1]
            waves.append(
                jnp.concatenate([p_re * o_re - p_im * o_im, p_re * o_im + p_im * o_re], axis=0)
            )
        wide = jnp.concatenate(waves, axis=1).astype(half)
        first = dot(left_f_ref[...], jnp.concatenate([wide, wide], axis=0)).astype(half)
        tall = jnp.concatenate(
            [
                jnp.concatenate(
                    [first[:PR, j * PC : (j + 1) * PC], first[PR:, j * PC : (j + 1) * PC]], axis=1
                )
                for j in range(CHUNK)
            ],
            axis=0,
        )
        far = dot(tall, right_f_ref[...])
        f_re, f_im = far[:, :PC], far[:, PC:]
        measured = measured_ref[0, pl.ds(chunk * CHUNK, CHUNK)].astype(jnp.float32)
        measured = measured.reshape(CHUNK * PR, PC)
        factor = 1.0 - jnp.sqrt(measured) * lax.rsqrt(f_re * f_re + f_im * f_im + 1.0)
        scaled = jnp.concatenate([f_re * factor, f_im * factor], axis=1).astype(half)
        second = dot(scaled, right_b_ref[...]).astype(half)
        wide = jnp.concatenate(
            [
                jnp.concatenate(
                    [second[j * PR : (j + 1) * PR, :PC], second[j * PR : (j + 1) * PR, PC:]], axis=0
                )
                for j in range(CHUNK)
            ],
            axis=1,
        )
        back = dot(left_b_ref[...], jnp.concatenate([wide, wide], axis=0))
        above = ext_rows - PR
        for j in range(CHUNK):
            shift = lax.rem(spots[j][1], PC)
            b_re = back[:PR, j * PC : (j + 1) * PC]
            b_im = back[PR:, j * PC : (j + 1) * PC]
            p_re, p_im = wave_ref[0], wave_ref[1]
            stage_ref[j, 0, above : above + PR] = pltpu.roll(p_re * b_re + p_im * b_im, shift, 1)
            stage_ref[j, 1, above : above + PR] = pltpu.roll(p_re * b_im - p_im * b_re, shift, 1)
        for channel in range(2):
            first_half = acc_ref[channel, 0]
            next_half = acc_ref[channel, 1]
            for j in range(CHUNK):
                row, col = spots[j]
                values = stage_ref[j, channel, pl.ds(above - row, ext_rows), :]
                first_half = first_half + jnp.where(wide_lane >= col, values, 0.0)
                next_half = next_half + jnp.where(wide_lane >= col, 0.0, values)
            acc_ref[channel, 0] = first_half
            acc_ref[channel, 1] = next_half
        return carry

    lax.fori_loop(0, 1, step, 0)

    for copy in id_copies:
        copy.wait_recv()
    id_local = pltpu.make_async_copy(all_ref, all_smem, local_sem.at[len(loads)])
    id_local.start()
    reach = own_blocks * part
    skew = lax.broadcasted_iota(jnp.int32, (part, reach), 1) - lax.broadcasted_iota(
        jnp.int32, (part, reach), 0
    )
    picks = []
    for n in range(places):
        q, r = divmod(n, capacity)
        want = jnp.concatenate([all_ref[q, r : r + 1, :]] * (reach // LANES), axis=1)
        picks.append(jnp.where(skew == want * part, 1.0, 0.0).astype(half))
    gathered = dot(jnp.concatenate(picks, axis=0), vol_half_ref[...].reshape(reach, PIX)).astype(half)
    for n in range(places):
        send_a[n] = gathered[n * part : (n + 1) * part]

    def exchange_copy(phase, d):
        peer = lax.rem(g + d, groups)
        return angle_copy(
            phase, d,
            sends[phase].at[pl.ds(peer * capacity, capacity)],
            recvs[phase].at[pl.ds(g * capacity, capacity)],
        )

    own = pl.ds(g * capacity, capacity)
    fetches = [exchange_copy(0, d) for d in rising]
    for copy in fetches:
        copy.start()
    recv_a[own] = send_a[own]

    lax.fori_loop(1, rows_ref.shape[1] // CHUNK, step, 0)

    rims = [[], []]
    grads = []
    for channel in (1, 0):
        for side in range(2):
            rim_ref[0, channel, :, lanes[side]] = acc_ref[channel, side, HALO + band :].astype(half)
            rim_ref[1, channel, :, lanes[side]] = acc_ref[channel, side, :HALO].astype(half)
        for way in range(2):
            where = {"tile": below if way == 0 else upper}
            across = dict(where, half=1 - h)
            index = 6 + way * 5 + channel * 2
            pair_of = [
                near(index, rim_ref.at[way, channel, away, :], rim_here_ref.at[way, h, channel], across),
                near(index + 1, rim_ref.at[way, channel, here, :], rim_here_ref.at[way, h, channel], where),
            ]
            rims[way].append(pair_of)

            def send(copies=pair_of):
                for copy in copies:
                    copy.start()

            when_sent(way, send)
        for side in range(2):
            grad_ref[channel, :, lanes[side]] = acc_ref[channel, side, HALO : HALO + band]
        grads.append(
            near(4 + channel, grad_ref.at[channel, away, :], both_grad_ref.at[h, channel], {"half": 1 - h})
        )
        grads[-1].start()
    for way in range(2):
        where = {"tile": below if way == 0 else upper}
        rims[way].append([near(10 + way * 5, rim_ref.at[way, :, away, :], rim_away_ref.at[way], where)])
        when_sent(way, rims[way][-1][0].start)
    both_grad_ref[h] = grad_ref[:, here, :]

    for copy in fetches:
        copy.wait_recv()
    loads[15].wait()

    def projected(phase, pair):
        total = jnp.zeros((part, RB), jnp.float32)
        for c in range(per_block):
            slot = pair * per_block + c
            picked = recvs[phase][place_ref[slot]]
            total = total + live_ref[slot] * lax.dot_general(
                picked, weight_ref[slot], (((1,), (1,)), ((), ())),
                preferred_element_type=jnp.float32,
            )
        return total

    sinos = [projected(0, pair) for pair in range(pairs)]

    def received(stage):
        for way in range(2):
            def take(copies=rims[way][stage]):
                for copy in copies:
                    copy.wait_recv()

            when_received(way, take)

    def renewed(angle, channel):
        around = both_grad_ref[angle, channel] + rim_here_ref[0, angle, channel].astype(jnp.float32)
        around = around + rim_here_ref[1, angle, channel].astype(jnp.float32)
        return both_base_ref[angle, channel] - descent * around

    base_copy.wait_recv()
    mult_copy.wait_recv()
    grads[0].wait_recv()
    received(0)
    news = [renewed(angle, 1) for angle in range(angles)]
    for pair in range(pairs):
        angle, k = divmod(pair, NRB)
        rays = slice(k * RB, (k + 1) * RB)
        target = news[angle][:, rays] + both_mult_ref[angle, 1, :, rays] / penalty
        residual_ref[pair] = (sinos[pair] - target).astype(half)

    def spread(n):
        slot = slot_ref[n]
        term = dot(residual_ref[lax.div(slot, per_block)], weight_ref[slot])
        return (used_ref[n] * term).astype(half)

    terms = []
    for d in paired:
        peer = lax.rem(g + d, groups)
        for r in range(capacity):
            send_b[peer * capacity + r] = spread(peer * capacity + r)
        terms.append(exchange_copy(1, d))
        terms[-1].start()
    for r in range(capacity):
        recv_b[g * capacity + r] = spread(g * capacity + r)

    width = places * part
    per_tile = LANES // part
    tile_lane = lax.broadcasted_iota(jnp.int32, (1, LANES), 1)
    keys = []
    for first in range(0, places, per_tile):
        key = jnp.zeros((1, LANES), jnp.int32)
        for n in range(first, first + per_tile):
            q, r = divmod(n, capacity)
            key = jnp.where(tile_lane // part == n - first, all_ref[q, r : r + 1, :], key)
        keys.append(key * part + tile_lane % part)
    key = jnp.concatenate(keys, axis=1)
    merge_ref[...] = jnp.where(
        lax.broadcasted_iota(jnp.int32, (reach, width), 0) == key, 1.0, 0.0
    ).astype(half)

    grads[1].wait_recv()
    received(1)
    received(2)
    for angle in range(angles):
        new_mult_ref[angle, 0] = both_mult_ref[angle, 0] + penalty * (renewed(angle, 0) - 1.0)
    for channel in range(2):
        updated_ref[0, channel, here, :] = renewed(h, channel)
        far = grad_ref[channel, away, :] + rim_away_ref[0, channel].astype(jnp.float32)
        far = far + rim_away_ref[1, channel].astype(jnp.float32)
        updated_ref[0, channel, away, :] = base_ref[channel, away, :] - descent * far
    id_local.wait()
    for copy in terms:
        copy.wait_recv()
    total = dot(merge_ref[...], recv_b[...].reshape(width, PIX)).reshape(own_blocks, part, PIX)
    block = vol_ref[...]
    new_vol = block - volume_step * (total + damping * block)
    new_vol_ref[...] = new_vol
    vol_half_ref[...] = new_vol.astype(half)
    renewals = []
    for d in paired:
        peer = lax.rem(g + d, groups)
        for r in range(capacity):
            send_c[peer * capacity + r] = vol_half_ref[all_smem[peer, r, 0]]
        renewals.append(exchange_copy(2, d))
        renewals[-1].start()
    for r in range(capacity):
        recv_c[g * capacity + r] = vol_half_ref[all_smem[g, r, 0]]
    for copy in renewals:
        copy.wait_recv()
    for pair in range(pairs):
        angle, k = divmod(pair, NRB)
        rays = slice(k * RB, (k + 1) * RB)
        fresh = projected(2, pair)
        new_mult_ref[angle, 1, :, rays] = both_mult_ref[angle, 1, :, rays] + penalty * (
            news[angle][:, rays] - fresh
        )
    for copy in id_copies + fetches + terms + renewals + grads + [base_copy, mult_copy]:
        copy.wait_send()
    for way in range(2):
        def settle(copies=sum(rims[way], [halo[way]])):
            for copy in copies:
                copy.wait_send()

        when_sent(way, settle)


def admm_step(ray_blocks, counts, rows, cols, own, multiplier, prior, measured, field, mask, volume, weights):
    groups = lax.axis_size("angle")
    tiles = lax.axis_size("tile")
    slots = ray_blocks.size
    capacity = max(2, -(-slots // groups))
    places = groups * capacity
    left_f, right_f = dft_blocks(-1.0)
    left_b, right_b = dft_blocks(1.0)
    left_f, left_b = (split_table(m) for m in (left_f, left_b))
    tables = [left_f, jnp.asarray(right_f, jnp.bfloat16), left_b, jnp.asarray(right_b, jnp.bfloat16)]
    vmem = pl.BlockSpec(memory_space=pltpu.VMEM)
    band = own.shape[2]
    part = band // 2
    assert band == HALO and capacity <= ROWS
    ext_rows = band + 2 * HALO
    own_blocks = volume.shape[0]
    block = volume.shape[1:]
    weights = weights.reshape((slots,) + weights.shape[3:])
    f32 = jnp.float32
    half = jnp.bfloat16
    operands = [
        ray_blocks, counts, rows, cols, own, multiplier, prior, field, mask, *tables,
        measured, volume, weights,
    ]
    spaces = [pltpu.SMEM] * 4 + [pltpu.VMEM] * 12
    return pl.pallas_call(
        functools.partial(step_kernel, groups, tiles, capacity),
        out_shape=(
            jax.ShapeDtypeStruct(own.shape, f32),
            jax.ShapeDtypeStruct(volume.shape, f32),
            jax.ShapeDtypeStruct((2, 2, part, NW), f32),
        ),
        in_specs=[pl.BlockSpec(memory_space=pltpu.HBM)] * 16,
        out_specs=(vmem, vmem, vmem),
        scratch_shapes=[
            *[space(x.shape, x.dtype) for space, x in zip(spaces, operands)],
            pltpu.SMEM((groups, ROWS, LANES), jnp.int32),
            pltpu.SMEM((slots,), jnp.int32),
            pltpu.SMEM((slots,), jnp.int32),
            pltpu.SMEM((places,), jnp.int32),
            pltpu.SMEM((places,), f32),
            pltpu.SMEM((slots,), f32),
            pltpu.VMEM((groups, ROWS, LANES), jnp.int32),
            pltpu.VMEM((groups, ROWS, LANES), jnp.int32),
            pltpu.VMEM((2, HALO, NW), half),
            pltpu.VMEM((2, HALO, NW), half),
            pltpu.VMEM((2, HALO, NW), half),
            pltpu.VMEM((2, NW // PC, ext_rows, PC), f32),
            pltpu.VMEM((2, NW // PC, ext_rows, PC), f32),
            pltpu.VMEM((2, PR, PC), f32),
            pltpu.VMEM((CHUNK, 2, 2 * (ext_rows - PR) + PR, PC), f32),
            pltpu.VMEM((2, band, NW), f32),
            pltpu.VMEM((2, band, NW), f32),
            *[pltpu.VMEM((2, 2, part, NW), f32)] * 3,
            pltpu.VMEM((2, 2, HALO, NW), half),
            pltpu.VMEM((2, 2, 2, part, NW), half),
            pltpu.VMEM((2, 2, part, NW), half),
            pltpu.VMEM((own_blocks,) + block, half),
            pltpu.VMEM((own_blocks * part, places * part), half),
            pltpu.VMEM((slots // weights_per_block(ray_blocks), part, RB), half),
            *[pltpu.VMEM((places,) + block, half)] * 6,
            pltpu.SemaphoreType.DMA((4, groups)),
            pltpu.SemaphoreType.DMA((4, groups)),
            pltpu.SemaphoreType.DMA((16,)),
            pltpu.SemaphoreType.DMA((16,)),
            pltpu.SemaphoreType.DMA((17,)),
        ],
        compiler_params=pltpu.CompilerParams(
            collective_id=1, has_side_effects=True, vmem_limit_bytes=32 * 1024 * 1024
        ),
    )(*operands)


def weights_per_block(ray_blocks):
    return ray_blocks.shape[2]


def write_kernel(a_ref, b_ref, c_ref, a_out, b_out, c_out, sems):
    copies = [
        pltpu.make_async_copy(source, target, sems.at[i])
        for i, (source, target) in enumerate(((a_ref, a_out), (b_ref, b_out), (c_ref, c_out)))
    ]
    for copy in copies:
        copy.start()
    for copy in copies:
        copy.wait()


def write_out(values):
    return pl.pallas_call(
        write_kernel,
        out_shape=tuple(jax.ShapeDtypeStruct(v.shape, v.dtype) for v in values),
        in_specs=[pl.BlockSpec(memory_space=pltpu.VMEM)] * 3,
        out_specs=tuple([pl.BlockSpec(memory_space=pl.ANY)] * 3),
        scratch_shapes=[pltpu.SemaphoreType.DMA((3,))],
    )(*values)


def shards(
    projection,
    multiplier,
    reprojection,
    intensity,
    row_start,
    column_start,
    probe_field,
    probe_mask,
    weights,
    ray_blocks,
    ray_counts,
    volume,
):
    return write_out(
        admm_step(
            ray_blocks, ray_counts, row_start, column_start, projection, multiplier, reprojection,
            intensity, probe_field, probe_mask, volume, weights,
        )
    )


def solution(mesh):
    return jax.shard_map(
        shards,
        mesh=mesh,
        in_specs=(
            P(("angle", "half"), None, "tile", None),
            P(("angle", "half"), None, "tile", None),
            P(("angle", "half"), "tile", None),
            P(("angle", "half"), "tile", None, None),
            P(("angle", "half"), "tile"),
            P(("angle", "half"), "tile"),
            P(),
            P(),
            P("angle", None, None, None, None),
            P("angle", None, None),
            P("angle", None),
            P("angle", ("tile", "half"), None),
        ),
        out_specs=(
            P(("angle", "half"), None, "tile", None),
            P("angle", ("tile", "half"), None),
            P("angle", None, ("tile", "half"), None),
        ),
        check_vma=False,
    )
```

```python
import functools

import jax
import jax.numpy as jnp
import numpy as np
from jax import lax
from jax.experimental import pallas as pl
from jax.experimental.pallas import tpu as pltpu
from jax.sharding import PartitionSpec as P

PR = 64
PC = 128
NW = 256
PIX = 512
RB = 128
CMAX = 4
HALO = 32
NRB = 2


penalty = 0.5
descent = 0.25
volume_step = 1.0
damping = 0.1


def dft_blocks(sign):
    def table(length):
        counter = np.arange(length)
        phase = (counter[:, None] * counter[None, :] % length) * (2.0 * np.pi / length)
        return np.cos(phase) / np.sqrt(length), sign * np.sin(phase) / np.sqrt(length)

    row_cos, row_sin = table(PR)
    col_cos, col_sin = table(PC)
    left = np.block([[row_cos, -row_sin], [row_sin, row_cos]])
    right = np.block([[col_cos, col_sin], [-col_sin, col_cos]])
    return left.astype(np.float32), right.astype(np.float32)


def split_table(matrix):
    coarse = matrix.astype(jnp.bfloat16)
    rest = (matrix - coarse.astype(np.float32)).astype(jnp.bfloat16)
    return jnp.asarray(np.concatenate([coarse, rest], axis=1))


MESH = pl.DeviceIdType.MESH
CHUNK = 16
ROWS = 8
LANES = 128


def orders(groups):
    rising = list(range(1, groups))
    paired = []
    for d in range(1, groups // 2 + 1):
        paired += [groups - d] if 2 * d == groups else [groups - d, d]
    if groups % 2:
        paired = rising
    return rising, paired


def step_kernel(
    groups, tiles, capacity,
    mine_hbm, counts_hbm, rows_hbm, cols_hbm, proj_hbm, mult_hbm, prior_hbm, field_hbm, mask_hbm,
    left_f_hbm, right_f_hbm, left_b_hbm, right_b_hbm, measured_hbm, vol_hbm, weight_hbm,
    updated_ref, new_vol_ref, new_mult_ref,
    mine_ref, counts_ref, rows_ref, cols_ref, proj_ref, mult_ref, prior_ref, field_ref, mask_ref,
    left_f_ref, right_f_ref, left_b_ref, right_b_ref, measured_ref, vol_ref, weight_ref,
    all_smem, place_ref, inside_ref, slot_ref, used_ref, live_ref,
    ids_ref, all_ref, edge_ref, before_ref, after_ref,
    ext_ref, acc_ref, wave_ref, stage_ref,
    base_ref, grad_ref, both_base_ref, both_mult_ref, both_grad_ref,
    rim_ref, rim_here_ref, rim_away_ref,
    vol_half_ref, merge_ref, residual_ref,
    send_a, send_b, send_c, recv_a, recv_b, recv_c,
    send_sem, recv_sem, near_send, near_recv, local_sem,
):
    g = lax.axis_index("angle")
    t = lax.axis_index("tile")
    h = lax.axis_index("half")
    band = proj_ref.shape[2]
    part = band // 2
    places = groups * capacity
    own_blocks = vol_ref.shape[0]
    angles, blocks, per_block = mine_ref.shape
    slots = angles * blocks * per_block
    pairs = slots // per_block
    has_up = t > 0
    has_down = t < tiles - 1
    half = jnp.bfloat16
    sends = (send_a, send_b, send_c)
    recvs = (recv_a, recv_b, recv_c)
    lanes = [slice(0, PC), slice(PC, NW)]
    rising, paired = orders(groups)

    def where_of(slot):
        pair, c = divmod(slot, per_block)
        angle, block = divmod(pair, blocks)
        return angle, block, c

    barrier = pltpu.get_barrier_semaphore()

    def greet(where):
        pl.semaphore_signal(barrier, inc=1, device_id=where, device_id_type=MESH)

    for d in rising:
        greet({"angle": lax.rem(g + d, groups)})
    greet({"half": 1 - h})

    @pl.when(has_up)
    def _():
        greet({"tile": t - 1})
        greet({"tile": t - 1, "half": 1 - h})

    @pl.when(has_down)
    def _():
        greet({"tile": t + 1})
        greet({"tile": t + 1, "half": 1 - h})

    sources = (
        mine_hbm, counts_hbm, rows_hbm, cols_hbm, proj_hbm, mult_hbm, prior_hbm, field_hbm, mask_hbm,
        left_f_hbm, right_f_hbm, left_b_hbm, right_b_hbm, measured_hbm, vol_hbm, weight_hbm,
    )
    targets = (
        mine_ref, counts_ref, rows_ref, cols_ref, proj_ref, mult_ref, prior_ref, field_ref, mask_ref,
        left_f_ref, right_f_ref, left_b_ref, right_b_ref, measured_ref, vol_ref, weight_ref,
    )
    loads = [
        pltpu.make_async_copy(source, target, local_sem.at[i])
        for i, (source, target) in enumerate(zip(sources, targets))
    ]
    for load in loads:
        load.start()

    @pl.when(jnp.logical_not(has_up))
    def _():
        before_ref[...] = jnp.zeros_like(before_ref)
        rim_here_ref[0] = jnp.zeros(rim_here_ref.shape[1:], half)
        rim_away_ref[0] = jnp.zeros(rim_away_ref.shape[1:], half)

    @pl.when(jnp.logical_not(has_down))
    def _():
        after_ref[...] = jnp.zeros_like(after_ref)
        rim_here_ref[1] = jnp.zeros(rim_here_ref.shape[1:], half)
        rim_away_ref[1] = jnp.zeros(rim_away_ref.shape[1:], half)

    acc_ref[...] = jnp.zeros_like(acc_ref)
    stage_ref[...] = jnp.zeros_like(stage_ref)
    ids_ref[...] = jnp.zeros_like(ids_ref)

    for load in loads[:2]:
        load.wait()
    blocks_of = [mine_ref[where_of(s)] for s in range(slots)]
    owners = [lax.div(b, own_blocks) for b in blocks_of]
    for s in range(slots):
        rank = jnp.int32(0)
        for earlier in range(s):
            rank = rank + jnp.where(owners[earlier] == owners[s], 1, 0)
        place_ref[s] = owners[s] * capacity + rank
        inside_ref[s] = lax.rem(blocks_of[s], own_blocks)
        angle, block, c = where_of(s)
        live_ref[s] = jnp.where(c < counts_ref[angle, block], 1.0, 0.0)

    def slot_of(n, carry):
        slot = jnp.int32(0)
        used = jnp.float32(0.0)
        for s in range(slots):
            hit = place_ref[s] == n
            slot = jnp.where(hit, s, slot)
            used = jnp.where(hit, live_ref[s], used)
        slot_ref[n] = slot
        used_ref[n] = used
        return carry

    lax.fori_loop(0, places, slot_of, 0)
    for n in range(places):
        q, r = divmod(n, capacity)
        ids_ref[q, r : r + 1, :] = jnp.full((1, LANES), inside_ref[slot_ref[n]], jnp.int32)

    away = pl.ds(pl.multiple_of((1 - h) * part, part), part)
    here = pl.ds(pl.multiple_of(h * part, part), part)
    for load in loads[4:9]:
        load.wait()
    edge_ref[...] = proj_ref[0].astype(half)
    for channel in range(2):
        old = proj_ref[0, channel]
        held = 1.0 if channel == 0 else prior_ref[0]
        base_ref[channel] = old - descent * (penalty * (old - held) + mult_ref[0, channel])
    for side in range(2):
        ext_ref[:, side, HALO : HALO + band] = proj_ref[0, :, :, lanes[side]]
    mask = mask_ref[...].astype(jnp.float32)
    wave_ref[0] = field_ref[0] * mask
    wave_ref[1] = field_ref[1] * mask
    both_base_ref[h] = base_ref[:, here, :]
    both_mult_ref[h] = mult_ref[0, :, here, :]
    loads[14].wait()
    vol_half_ref[...] = vol_ref[...].astype(half)

    pl.semaphore_wait(
        barrier, groups + 2 * has_up.astype(jnp.int32) + 2 * has_down.astype(jnp.int32)
    )

    def angle_copy(phase, d, source, target):
        return pltpu.make_async_remote_copy(
            src_ref=source,
            dst_ref=target,
            send_sem=send_sem.at[phase, d],
            recv_sem=recv_sem.at[phase, d],
            device_id={"angle": lax.rem(g + d, groups)},
            device_id_type=MESH,
        )

    def near(index, source, target, where):
        return pltpu.make_async_remote_copy(
            src_ref=source,
            dst_ref=target,
            send_sem=near_send.at[index],
            recv_sem=near_recv.at[index],
            device_id=where,
            device_id_type=MESH,
        )

    below = jnp.minimum(t + 1, tiles - 1)
    upper = jnp.maximum(t - 1, 0)

    def when_sent(way, act):
        pl.when(has_down if way == 0 else has_up)(act)

    def when_received(way, act):
        pl.when(has_up if way == 0 else has_down)(act)

    id_copies = [
        angle_copy(3, d, ids_ref.at[lax.rem(g + d, groups)], all_ref.at[g]) for d in rising
    ]
    for copy in id_copies:
        copy.start()
    halo = [
        near(0, edge_ref, before_ref, {"tile": below}),
        near(1, edge_ref, after_ref, {"tile": upper}),
    ]
    for way in range(2):
        when_sent(way, halo[way].start)
    base_copy = near(2, base_ref.at[:, away, :], both_base_ref.at[h], {"half": 1 - h})
    mult_copy = near(3, mult_ref.at[0, :, away, :], both_mult_ref.at[h], {"half": 1 - h})
    base_copy.start()
    mult_copy.start()
    all_ref[g] = ids_ref[g]
    for load in loads[2:4] + loads[9:14]:
        load.wait()
    for way in range(2):
        when_received(way, halo[way].wait_recv)
    for side in range(2):
        ext_ref[:, side, :HALO] = before_ref[:, :, lanes[side]].astype(jnp.float32)
        ext_ref[:, side, HALO + band :] = after_ref[:, :, lanes[side]].astype(jnp.float32)

    lane = lax.broadcasted_iota(jnp.int32, (PR, PC), 1)
    ext_rows = band + 2 * HALO
    wide_lane = lax.broadcasted_iota(jnp.int32, (ext_rows, PC), 1)

    def dot(a, b):
        return jnp.dot(a, b, preferred_element_type=jnp.float32)

    def step(chunk, carry):
        waves = []
        spots = []
        for j in range(CHUNK):
            p = chunk * CHUNK + j
            row = rows_ref[0, p] + HALO
            col = cols_ref[0, p]
            spots.append((row, col))
            back_shift = lax.rem(NW - col, PC)

            def window(channel):
                near = pltpu.roll(ext_ref[channel, 0, pl.ds(row, PR), :], back_shift, 1)
                next_ = pltpu.roll(ext_ref[channel, 1, pl.ds(row, PR), :], back_shift, 1)
                return jnp.where(lane + col < PC, near, next_)

            o_re = window(0)
            o_im = window(1)
            p_re, p_im = wave_ref[0], wave_ref[1]
            waves.append(
                jnp.concatenate([p_re * o_re - p_im * o_im, p_re * o_im + p_im * o_re], axis=0)
            )
        wide = jnp.concatenate(waves, axis=1).astype(half)
        first = dot(left_f_ref[...], jnp.concatenate([wide, wide], axis=0)).astype(half)
        tall = jnp.concatenate(
            [
                jnp.concatenate(
                    [first[:PR, j * PC : (j + 1) * PC], first[PR:, j * PC : (j + 1) * PC]], axis=1
                )
                for j in range(CHUNK)
            ],
            axis=0,
        )
        far = dot(tall, right_f_ref[...])
        f_re, f_im = far[:, :PC], far[:, PC:]
        measured = measured_ref[0, pl.ds(chunk * CHUNK, CHUNK)].astype(jnp.float32)
        measured = measured.reshape(CHUNK * PR, PC)
        factor = 1.0 - jnp.sqrt(measured) * lax.rsqrt(f_re * f_re + f_im * f_im + 1.0)
        scaled = jnp.concatenate([f_re * factor, f_im * factor], axis=1).astype(half)
        second = dot(scaled, right_b_ref[...]).astype(half)
        wide = jnp.concatenate(
            [
                jnp.concatenate(
                    [second[j * PR : (j + 1) * PR, :PC], second[j * PR : (j + 1) * PR, PC:]], axis=0
                )
                for j in range(CHUNK)
            ],
            axis=1,
        )
        back = dot(left_b_ref[...], jnp.concatenate([wide, wide], axis=0))
        above = ext_rows - PR
        for j in range(CHUNK):
            shift = lax.rem(spots[j][1], PC)
            b_re = back[:PR, j * PC : (j + 1) * PC]
            b_im = back[PR:, j * PC : (j + 1) * PC]
            p_re, p_im = wave_ref[0], wave_ref[1]
            stage_ref[j, 0, above : above + PR] = pltpu.roll(p_re * b_re + p_im * b_im, shift, 1)
            stage_ref[j, 1, above : above + PR] = pltpu.roll(p_re * b_im - p_im * b_re, shift, 1)
        for channel in range(2):
            first_half = acc_ref[channel, 0]
            next_half = acc_ref[channel, 1]
            for j in range(CHUNK):
                row, col = spots[j]
                values = stage_ref[j, channel, pl.ds(above - row, ext_rows), :]
                first_half = first_half + jnp.where(wide_lane >= col, values, 0.0)
                next_half = next_half + jnp.where(wide_lane >= col, 0.0, values)
            acc_ref[channel, 0] = first_half
            acc_ref[channel, 1] = next_half
        return carry

    lax.fori_loop(0, 1, step, 0)

    for copy in id_copies:
        copy.wait_recv()
    id_local = pltpu.make_async_copy(all_ref, all_smem, local_sem.at[len(loads)])
    id_local.start()
    reach = own_blocks * part
    skew = lax.broadcasted_iota(jnp.int32, (part, reach), 1) - lax.broadcasted_iota(
        jnp.int32, (part, reach), 0
    )
    picks = []
    for n in range(places):
        q, r = divmod(n, capacity)
        want = jnp.concatenate([all_ref[q, r : r + 1, :]] * (reach // LANES), axis=1)
        picks.append(jnp.where(skew == want * part, 1.0, 0.0).astype(half))
    gathered = dot(jnp.concatenate(picks, axis=0), vol_half_ref[...].reshape(reach, PIX)).astype(half)
    for n in range(places):
        send_a[n] = gathered[n * part : (n + 1) * part]

    def exchange_copy(phase, d):
        peer = lax.rem(g + d, groups)
        return angle_copy(
            phase, d,
            sends[phase].at[pl.ds(peer * capacity, capacity)],
            recvs[phase].at[pl.ds(g * capacity, capacity)],
        )

    own = pl.ds(g * capacity, capacity)
    fetches = [exchange_copy(0, d) for d in rising]
    for copy in fetches:
        copy.start()
    recv_a[own] = send_a[own]

    lax.fori_loop(1, rows_ref.shape[1] // CHUNK, step, 0)

    rims = [[], []]
    grads = []
    for channel in (1, 0):
        for side in range(2):
            rim_ref[0, channel, :, lanes[side]] = acc_ref[channel, side, HALO + band :].astype(half)
            rim_ref[1, channel, :, lanes[side]] = acc_ref[channel, side, :HALO].astype(half)
        for way in range(2):
            where = {"tile": below if way == 0 else upper}
            across = dict(where, half=1 - h)
            index = 6 + way * 5 + channel * 2
            pair_of = [
                near(index, rim_ref.at[way, channel, away, :], rim_here_ref.at[way, h, channel], across),
                near(index + 1, rim_ref.at[way, channel, here, :], rim_here_ref.at[way, h, channel], where),
            ]
            rims[way].append(pair_of)

            def send(copies=pair_of):
                for copy in copies:
                    copy.start()

            when_sent(way, send)
        for side in range(2):
            grad_ref[channel, :, lanes[side]] = acc_ref[channel, side, HALO : HALO + band]
        grads.append(
            near(4 + channel, grad_ref.at[channel, away, :], both_grad_ref.at[h, channel], {"half": 1 - h})
        )
        grads[-1].start()
    for way in range(2):
        where = {"tile": below if way == 0 else upper}
        rims[way].append([near(10 + way * 5, rim_ref.at[way, :, away, :], rim_away_ref.at[way], where)])
        when_sent(way, rims[way][-1][0].start)
    both_grad_ref[h] = grad_ref[:, here, :]

    for copy in fetches:
        copy.wait_recv()
    loads[15].wait()

    def projected(phase, pair):
        total = jnp.zeros((part, RB), jnp.float32)
        for c in range(per_block):
            slot = pair * per_block + c
            picked = recvs[phase][place_ref[slot]]
            total = total + live_ref[slot] * lax.dot_general(
                picked, weight_ref[slot], (((1,), (1,)), ((), ())),
                preferred_element_type=jnp.float32,
            )
        return total

    sinos = [projected(0, pair) for pair in range(pairs)]

    def received(stage):
        for way in range(2):
            def take(copies=rims[way][stage]):
                for copy in copies:
                    copy.wait_recv()

            when_received(way, take)

    def renewed(angle, channel):
        around = both_grad_ref[angle, channel] + rim_here_ref[0, angle, channel].astype(jnp.float32)
        around = around + rim_here_ref[1, angle, channel].astype(jnp.float32)
        return both_base_ref[angle, channel] - descent * around

    base_copy.wait_recv()
    mult_copy.wait_recv()
    grads[0].wait_recv()
    received(0)
    news = [renewed(angle, 1) for angle in range(angles)]
    for pair in range(pairs):
        angle, k = divmod(pair, NRB)
        rays = slice(k * RB, (k + 1) * RB)
        target = news[angle][:, rays] + both_mult_ref[angle, 1, :, rays] / penalty
        residual_ref[pair] = (sinos[pair] - target).astype(half)

    def spread(n):
        slot = slot_ref[n]
        term = dot(residual_ref[lax.div(slot, per_block)], weight_ref[slot])
        return (used_ref[n] * term).astype(half)

    terms = []
    for d in paired:
        peer = lax.rem(g + d, groups)
        for r in range(capacity):
            send_b[peer * capacity + r] = spread(peer * capacity + r)
        terms.append(exchange_copy(1, d))
        terms[-1].start()
    for r in range(capacity):
        recv_b[g * capacity + r] = spread(g * capacity + r)

    width = places * part
    per_tile = LANES // part
    tile_lane = lax.broadcasted_iota(jnp.int32, (1, LANES), 1)
    keys = []
    for first in range(0, places, per_tile):
        key = jnp.zeros((1, LANES), jnp.int32)
        for n in range(first, first + per_tile):
            q, r = divmod(n, capacity)
            key = jnp.where(tile_lane // part == n - first, all_ref[q, r : r + 1, :], key)
        keys.append(key * part + tile_lane % part)
    key = jnp.concatenate(keys, axis=1)
    merge_ref[...] = jnp.where(
        lax.broadcasted_iota(jnp.int32, (reach, width), 0) == key, 1.0, 0.0
    ).astype(half)

    grads[1].wait_recv()
    received(1)
    received(2)
    for angle in range(angles):
        new_mult_ref[angle, 0] = both_mult_ref[angle, 0] + penalty * (renewed(angle, 0) - 1.0)
    for channel in range(2):
        updated_ref[0, channel, here, :] = renewed(h, channel)
        far = grad_ref[channel, away, :] + rim_away_ref[0, channel].astype(jnp.float32)
        far = far + rim_away_ref[1, channel].astype(jnp.float32)
        updated_ref[0, channel, away, :] = base_ref[channel, away, :] - descent * far
    id_local.wait()
    for copy in terms:
        copy.wait_recv()
    total = dot(merge_ref[...], recv_b[...].reshape(width, PIX)).reshape(own_blocks, part, PIX)
    block = vol_ref[...]
    new_vol = block - volume_step * (total + damping * block)
    new_vol_ref[...] = new_vol
    vol_half_ref[...] = new_vol.astype(half)
    renewals = []
    for d in paired:
        peer = lax.rem(g + d, groups)
        for r in range(capacity):
            send_c[peer * capacity + r] = vol_half_ref[all_smem[peer, r, 0]]
        renewals.append(exchange_copy(2, d))
        renewals[-1].start()
    for r in range(capacity):
        recv_c[g * capacity + r] = vol_half_ref[all_smem[g, r, 0]]
    for copy in renewals:
        copy.wait_recv()
    for pair in range(pairs):
        angle, k = divmod(pair, NRB)
        rays = slice(k * RB, (k + 1) * RB)
        fresh = projected(2, pair)
        new_mult_ref[angle, 1, :, rays] = both_mult_ref[angle, 1, :, rays] + penalty * (
            news[angle][:, rays] - fresh
        )
    for copy in id_copies + fetches + terms + renewals + grads + [base_copy, mult_copy]:
        copy.wait_send()
    for way in range(2):
        def settle(copies=sum(rims[way], [halo[way]])):
            for copy in copies:
                copy.wait_send()

        when_sent(way, settle)


def admm_step(ray_blocks, counts, rows, cols, own, multiplier, prior, measured, field, mask, volume, weights):
    groups = lax.axis_size("angle")
    tiles = lax.axis_size("tile")
    slots = ray_blocks.size
    capacity = max(2, -(-slots // groups))
    places = groups * capacity
    left_f, right_f = dft_blocks(-1.0)
    left_b, right_b = dft_blocks(1.0)
    left_f, left_b = (split_table(m) for m in (left_f, left_b))
    tables = [left_f, jnp.asarray(right_f, jnp.bfloat16), left_b, jnp.asarray(right_b, jnp.bfloat16)]
    vmem = pl.BlockSpec(memory_space=pltpu.VMEM)
    band = own.shape[2]
    part = band // 2
    assert band == HALO and capacity <= ROWS
    ext_rows = band + 2 * HALO
    own_blocks = volume.shape[0]
    block = volume.shape[1:]
    weights = weights.reshape((slots,) + weights.shape[3:])
    f32 = jnp.float32
    half = jnp.bfloat16
    operands = [
        ray_blocks, counts, rows, cols, own, multiplier, prior, field, mask, *tables,
        measured, volume, weights,
    ]
    spaces = [pltpu.SMEM] * 4 + [pltpu.VMEM] * 12
    return pl.pallas_call(
        functools.partial(step_kernel, groups, tiles, capacity),
        out_shape=(
            jax.ShapeDtypeStruct(own.shape, f32),
            jax.ShapeDtypeStruct(volume.shape, f32),
            jax.ShapeDtypeStruct((2, 2, part, NW), f32),
        ),
        in_specs=[pl.BlockSpec(memory_space=pltpu.HBM)] * 16,
        out_specs=(vmem, vmem, vmem),
        scratch_shapes=[
            *[space(x.shape, x.dtype) for space, x in zip(spaces, operands)],
            pltpu.SMEM((groups, ROWS, LANES), jnp.int32),
            pltpu.SMEM((slots,), jnp.int32),
            pltpu.SMEM((slots,), jnp.int32),
            pltpu.SMEM((places,), jnp.int32),
            pltpu.SMEM((places,), f32),
            pltpu.SMEM((slots,), f32),
            pltpu.VMEM((groups, ROWS, LANES), jnp.int32),
            pltpu.VMEM((groups, ROWS, LANES), jnp.int32),
            pltpu.VMEM((2, HALO, NW), half),
            pltpu.VMEM((2, HALO, NW), half),
            pltpu.VMEM((2, HALO, NW), half),
            pltpu.VMEM((2, NW // PC, ext_rows, PC), f32),
            pltpu.VMEM((2, NW // PC, ext_rows, PC), f32),
            pltpu.VMEM((2, PR, PC), f32),
            pltpu.VMEM((CHUNK, 2, 2 * (ext_rows - PR) + PR, PC), f32),
            pltpu.VMEM((2, band, NW), f32),
            pltpu.VMEM((2, band, NW), f32),
            *[pltpu.VMEM((2, 2, part, NW), f32)] * 3,
            pltpu.VMEM((2, 2, HALO, NW), half),
            pltpu.VMEM((2, 2, 2, part, NW), half),
            pltpu.VMEM((2, 2, part, NW), half),
            pltpu.VMEM((own_blocks,) + block, half),
            pltpu.VMEM((own_blocks * part, places * part), half),
            pltpu.VMEM((slots // weights_per_block(ray_blocks), part, RB), half),
            *[pltpu.VMEM((places,) + block, half)] * 6,
            pltpu.SemaphoreType.DMA((4, groups)),
            pltpu.SemaphoreType.DMA((4, groups)),
            pltpu.SemaphoreType.DMA((16,)),
            pltpu.SemaphoreType.DMA((16,)),
            pltpu.SemaphoreType.DMA((17,)),
        ],
        compiler_params=pltpu.CompilerParams(
            collective_id=1, has_side_effects=True, vmem_limit_bytes=32 * 1024 * 1024
        ),
    )(*[pltpu.with_memory_space_constraint(x, pltpu.HBM) for x in operands])


def weights_per_block(ray_blocks):
    return ray_blocks.shape[2]


def write_kernel(a_ref, b_ref, c_ref, a_out, b_out, c_out, sems):
    copies = [
        pltpu.make_async_copy(source, target, sems.at[i])
        for i, (source, target) in enumerate(((a_ref, a_out), (b_ref, b_out), (c_ref, c_out)))
    ]
    for copy in copies:
        copy.start()
    for copy in copies:
        copy.wait()


def write_out(values):
    return pl.pallas_call(
        write_kernel,
        out_shape=tuple(jax.ShapeDtypeStruct(v.shape, v.dtype) for v in values),
        in_specs=[pl.BlockSpec(memory_space=pltpu.VMEM)] * 3,
        out_specs=tuple([pl.BlockSpec(memory_space=pl.ANY)] * 3),
        scratch_shapes=[pltpu.SemaphoreType.DMA((3,))],
        compiler_params=pltpu.CompilerParams(vmem_limit_bytes=8 * 1024 * 1024),
    )(*values)


def shards(
    projection,
    multiplier,
    reprojection,
    intensity,
    row_start,
    column_start,
    probe_field,
    probe_mask,
    weights,
    ray_blocks,
    ray_counts,
    volume,
):
    return write_out(
        admm_step(
            ray_blocks, ray_counts, row_start, column_start, projection, multiplier, reprojection,
            intensity, probe_field, probe_mask, volume, weights,
        )
    )


def solution(mesh):
    return jax.shard_map(
        shards,
        mesh=mesh,
        in_specs=(
            P(("angle", "half"), None, "tile", None),
            P(("angle", "half"), None, "tile", None),
            P(("angle", "half"), "tile", None),
            P(("angle", "half"), "tile", None, None),
            P(("angle", "half"), "tile"),
            P(("angle", "half"), "tile"),
            P(),
            P(),
            P("angle", None, None, None, None),
            P("angle", None, None),
            P("angle", None),
            P("angle", ("tile", "half"), None),
        ),
        out_specs=(
            P(("angle", "half"), None, "tile", None),
            P("angle", ("tile", "half"), None),
            P("angle", None, ("tile", "half"), None),
        ),
        check_vma=False,
    )
```

```python
import functools

import jax
import jax.numpy as jnp
import numpy as np
from jax import lax
from jax.experimental import pallas as pl
from jax.experimental.pallas import tpu as pltpu
from jax.sharding import PartitionSpec as P

PR = 64
PC = 128
NW = 256
PIX = 512
RB = 128
CMAX = 4
HALO = 32
NRB = 2


penalty = 0.5
descent = 0.25
volume_step = 1.0
damping = 0.1


def dft_blocks(sign):
    def table(length):
        counter = np.arange(length)
        phase = (counter[:, None] * counter[None, :] % length) * (2.0 * np.pi / length)
        return np.cos(phase) / np.sqrt(length), sign * np.sin(phase) / np.sqrt(length)

    row_cos, row_sin = table(PR)
    col_cos, col_sin = table(PC)
    left = np.block([[row_cos, -row_sin], [row_sin, row_cos]])
    right = np.block([[col_cos, col_sin], [-col_sin, col_cos]])
    return left.astype(np.float32), right.astype(np.float32)


def split_table(matrix):
    coarse = matrix.astype(jnp.bfloat16)
    rest = (matrix - coarse.astype(np.float32)).astype(jnp.bfloat16)
    return jnp.asarray(np.concatenate([coarse, rest], axis=1))


MESH = pl.DeviceIdType.MESH
CHUNK = 16
ROWS = 8
LANES = 128


def orders(groups):
    rising = list(range(1, groups))
    return rising, [groups // 2] + [d for d in reversed(rising) if 2 * d != groups]


def flipped(index, mask, count):
    out = jnp.int32(0)
    bit = 1
    while bit < count:
        out = out + lax.rem(lax.div(index, bit) + mask // bit, 2) * bit
        bit *= 2
    return out


def step_kernel(
    groups, tiles, capacity,
    mine_hbm, counts_hbm, rows_hbm, cols_hbm, proj_hbm, mult_hbm, prior_hbm, field_hbm, mask_hbm,
    left_f_hbm, right_f_hbm, left_b_hbm, right_b_hbm, measured_hbm, vol_hbm, weight_hbm,
    updated_ref, new_vol_ref, new_mult_ref,
    mine_ref, counts_ref, rows_ref, cols_ref, proj_ref, mult_ref, prior_ref, field_ref, mask_ref,
    left_f_ref, right_f_ref, left_b_ref, right_b_ref, measured_ref, vol_ref, weight_ref,
    all_smem, place_ref, inside_ref, slot_ref, used_ref, live_ref,
    ids_ref, all_ref, edge_ref, before_ref, after_ref,
    ext_ref, acc_ref, wave_ref, stage_ref,
    base_ref, grad_ref, both_base_ref, both_mult_ref, both_grad_ref,
    rim_ref, rim_here_ref, rim_away_ref,
    vol_half_ref, merge_ref, residual_ref,
    tile_ref, far_tile_ref, twin_send_ref, twin_recv_ref, part_send_ref, part_recv_ref,
    send_a, send_b, send_c, recv_a, recv_b, recv_c,
    send_sem, recv_sem, near_send, near_recv, local_sem,
):
    g = lax.axis_index("angle")
    t = lax.axis_index("tile")
    h = lax.axis_index("half")
    band = proj_ref.shape[2]
    part = band // 2
    places = groups * capacity
    own_blocks = vol_ref.shape[0]
    angles, blocks, per_block = mine_ref.shape
    slots = angles * blocks * per_block
    pairs = slots // per_block
    has_up = t > 0
    has_down = t < tiles - 1
    half = jnp.bfloat16
    sends = (send_a, send_b, send_c)
    recvs = (recv_a, recv_b, recv_c)
    lanes = [slice(0, PC), slice(PC, NW)]
    rising, paired = orders(groups)
    peers = {m: flipped(g, m, groups) for m in rising}
    across = groups // 2
    twin = lax.rem(g + across, groups)
    column = lax.rem(t, 2)
    quarter = RB // 4

    def where_of(slot):
        pair, c = divmod(slot, per_block)
        angle, block = divmod(pair, blocks)
        return angle, block, c

    barrier = pltpu.get_barrier_semaphore()

    def greet(where):
        pl.semaphore_signal(barrier, inc=1, device_id=where, device_id_type=MESH)

    for d in rising:
        greet({"angle": peers[d]})
    greet({"half": 1 - h})

    @pl.when(has_up)
    def _():
        greet({"tile": t - 1})
        greet({"tile": t - 1, "half": 1 - h})

    @pl.when(has_down)
    def _():
        greet({"tile": t + 1})
        greet({"tile": t + 1, "half": 1 - h})

    sources = (
        mine_hbm, counts_hbm, rows_hbm, cols_hbm, proj_hbm, mult_hbm, prior_hbm, field_hbm, mask_hbm,
        left_f_hbm, right_f_hbm, left_b_hbm, right_b_hbm, measured_hbm, vol_hbm, weight_hbm,
    )
    targets = (
        mine_ref, counts_ref, rows_ref, cols_ref, proj_ref, mult_ref, prior_ref, field_ref, mask_ref,
        left_f_ref, right_f_ref, left_b_ref, right_b_ref, measured_ref, vol_ref, weight_ref,
    )
    loads = [
        pltpu.make_async_copy(source, target, local_sem.at[i])
        for i, (source, target) in enumerate(zip(sources, targets))
    ]
    for load in loads:
        load.start()

    @pl.when(jnp.logical_not(has_up))
    def _():
        before_ref[...] = jnp.zeros_like(before_ref)
        rim_here_ref[0] = jnp.zeros(rim_here_ref.shape[1:], half)
        rim_away_ref[0] = jnp.zeros(rim_away_ref.shape[1:], half)

    @pl.when(jnp.logical_not(has_down))
    def _():
        after_ref[...] = jnp.zeros_like(after_ref)
        rim_here_ref[1] = jnp.zeros(rim_here_ref.shape[1:], half)
        rim_away_ref[1] = jnp.zeros(rim_away_ref.shape[1:], half)

    acc_ref[...] = jnp.zeros_like(acc_ref)
    stage_ref[...] = jnp.zeros_like(stage_ref)
    ids_ref[...] = jnp.zeros_like(ids_ref)

    for load in loads[:2]:
        load.wait()
    blocks_of = [mine_ref[where_of(s)] for s in range(slots)]
    owners = [lax.div(b, own_blocks) for b in blocks_of]
    for s in range(slots):
        rank = jnp.int32(0)
        for earlier in range(s):
            rank = rank + jnp.where(owners[earlier] == owners[s], 1, 0)
        place_ref[s] = owners[s] * capacity + rank
        inside_ref[s] = lax.rem(blocks_of[s], own_blocks)
        angle, block, c = where_of(s)
        live_ref[s] = jnp.where(c < counts_ref[angle, block], 1.0, 0.0)

    def slot_of(n, carry):
        slot = jnp.int32(0)
        used = jnp.float32(0.0)
        for s in range(slots):
            hit = place_ref[s] == n
            slot = jnp.where(hit, s, slot)
            used = jnp.where(hit, live_ref[s], used)
        slot_ref[n] = slot
        used_ref[n] = used
        return carry

    lax.fori_loop(0, places, slot_of, 0)
    for n in range(places):
        q, r = divmod(n, capacity)
        ids_ref[q, r : r + 1, :] = jnp.full((1, LANES), inside_ref[slot_ref[n]], jnp.int32)

    away = pl.ds(pl.multiple_of((1 - h) * part, part), part)
    here = pl.ds(pl.multiple_of(h * part, part), part)
    for load in loads[4:9]:
        load.wait()
    edge_ref[...] = proj_ref[0].astype(half)
    for channel in range(2):
        old = proj_ref[0, channel]
        held = 1.0 if channel == 0 else prior_ref[0]
        base_ref[channel] = old - descent * (penalty * (old - held) + mult_ref[0, channel])
    for side in range(2):
        ext_ref[:, side, HALO : HALO + band] = proj_ref[0, :, :, lanes[side]]
    mask = mask_ref[...].astype(jnp.float32)
    wave_ref[0] = field_ref[0] * mask
    wave_ref[1] = field_ref[1] * mask
    both_base_ref[h] = base_ref[:, here, :]
    both_mult_ref[h] = mult_ref[0, :, here, :]
    loads[14].wait()
    vol_half_ref[...] = vol_ref[...].astype(half)
    loads[15].wait()
    first_ray = pl.multiple_of((2 * h + column) * quarter, quarter)
    for r in range(capacity):
        tile_ref[r] = weight_ref[slot_ref[twin * capacity + r], pl.ds(first_ray, quarter), :]
        recv_c[twin * capacity + r] = jnp.zeros(recv_c.shape[1:], half)

    pl.semaphore_wait(
        barrier, groups + 2 * has_up.astype(jnp.int32) + 2 * has_down.astype(jnp.int32)
    )

    def angle_copy(phase, d, source, target):
        return pltpu.make_async_remote_copy(
            src_ref=source,
            dst_ref=target,
            send_sem=send_sem.at[phase, d],
            recv_sem=recv_sem.at[phase, d],
            device_id={"angle": peers[d]},
            device_id_type=MESH,
        )

    def near(index, source, target, where):
        return pltpu.make_async_remote_copy(
            src_ref=source,
            dst_ref=target,
            send_sem=near_send.at[index],
            recv_sem=near_recv.at[index],
            device_id=where,
            device_id_type=MESH,
        )

    below = jnp.minimum(t + 1, tiles - 1)
    upper = jnp.maximum(t - 1, 0)

    def when_sent(way, act):
        pl.when(has_down if way == 0 else has_up)(act)

    def when_received(way, act):
        pl.when(has_up if way == 0 else has_down)(act)

    id_copies = [
        angle_copy(3, d, ids_ref.at[peers[d]], all_ref.at[g]) for d in rising
    ]
    for copy in id_copies:
        copy.start()
    tile_copy = angle_copy(4, across, tile_ref, far_tile_ref.at[h, column])
    tile_copy.start()
    halo = [
        near(0, edge_ref, before_ref, {"tile": below}),
        near(1, edge_ref, after_ref, {"tile": upper}),
    ]
    for way in range(2):
        when_sent(way, halo[way].start)
    base_copy = near(2, base_ref.at[:, away, :], both_base_ref.at[h], {"half": 1 - h})
    mult_copy = near(3, mult_ref.at[0, :, away, :], both_mult_ref.at[h], {"half": 1 - h})
    base_copy.start()
    mult_copy.start()
    all_ref[g] = ids_ref[g]
    for load in loads[2:4] + loads[9:14]:
        load.wait()
    for way in range(2):
        when_received(way, halo[way].wait_recv)
    for side in range(2):
        ext_ref[:, side, :HALO] = before_ref[:, :, lanes[side]].astype(jnp.float32)
        ext_ref[:, side, HALO + band :] = after_ref[:, :, lanes[side]].astype(jnp.float32)

    lane = lax.broadcasted_iota(jnp.int32, (PR, PC), 1)
    ext_rows = band + 2 * HALO
    wide_lane = lax.broadcasted_iota(jnp.int32, (ext_rows, PC), 1)

    def dot(a, b):
        return jnp.dot(a, b, preferred_element_type=jnp.float32)

    def step(chunk, carry):
        waves = []
        spots = []
        for j in range(CHUNK):
            p = chunk * CHUNK + j
            row = rows_ref[0, p] + HALO
            col = cols_ref[0, p]
            spots.append((row, col))
            back_shift = lax.rem(NW - col, PC)

            def window(channel):
                near = pltpu.roll(ext_ref[channel, 0, pl.ds(row, PR), :], back_shift, 1)
                next_ = pltpu.roll(ext_ref[channel, 1, pl.ds(row, PR), :], back_shift, 1)
                return jnp.where(lane + col < PC, near, next_)

            o_re = window(0)
            o_im = window(1)
            p_re, p_im = wave_ref[0], wave_ref[1]
            waves.append(
                jnp.concatenate([p_re * o_re - p_im * o_im, p_re * o_im + p_im * o_re], axis=0)
            )
        wide = jnp.concatenate(waves, axis=1).astype(half)
        first = dot(left_f_ref[...], jnp.concatenate([wide, wide], axis=0)).astype(half)
        tall = jnp.concatenate(
            [
                jnp.concatenate(
                    [first[:PR, j * PC : (j + 1) * PC], first[PR:, j * PC : (j + 1) * PC]], axis=1
                )
                for j in range(CHUNK)
            ],
            axis=0,
        )
        far = dot(tall, right_f_ref[...])
        f_re, f_im = far[:, :PC], far[:, PC:]
        measured = measured_ref[0, pl.ds(chunk * CHUNK, CHUNK)].astype(jnp.float32)
        measured = measured.reshape(CHUNK * PR, PC)
        factor = 1.0 - jnp.sqrt(measured) * lax.rsqrt(f_re * f_re + f_im * f_im + 1.0)
        scaled = jnp.concatenate([f_re * factor, f_im * factor], axis=1).astype(half)
        second = dot(scaled, right_b_ref[...]).astype(half)
        wide = jnp.concatenate(
            [
                jnp.concatenate(
                    [second[j * PR : (j + 1) * PR, :PC], second[j * PR : (j + 1) * PR, PC:]], axis=0
                )
                for j in range(CHUNK)
            ],
            axis=1,
        )
        back = dot(left_b_ref[...], jnp.concatenate([wide, wide], axis=0))
        above = ext_rows - PR
        for j in range(CHUNK):
            shift = lax.rem(spots[j][1], PC)
            b_re = back[:PR, j * PC : (j + 1) * PC]
            b_im = back[PR:, j * PC : (j + 1) * PC]
            p_re, p_im = wave_ref[0], wave_ref[1]
            stage_ref[j, 0, above : above + PR] = pltpu.roll(p_re * b_re + p_im * b_im, shift, 1)
            stage_ref[j, 1, above : above + PR] = pltpu.roll(p_re * b_im - p_im * b_re, shift, 1)
        for channel in range(2):
            first_half = acc_ref[channel, 0]
            next_half = acc_ref[channel, 1]
            for j in range(CHUNK):
                row, col = spots[j]
                values = stage_ref[j, channel, pl.ds(above - row, ext_rows), :]
                first_half = first_half + jnp.where(wide_lane >= col, values, 0.0)
                next_half = next_half + jnp.where(wide_lane >= col, 0.0, values)
            acc_ref[channel, 0] = first_half
            acc_ref[channel, 1] = next_half
        return carry

    lax.fori_loop(0, 1, step, 0)

    for copy in id_copies:
        copy.wait_recv()
    id_local = pltpu.make_async_copy(all_ref, all_smem, local_sem.at[len(loads)])
    id_local.start()
    reach = own_blocks * part
    skew = lax.broadcasted_iota(jnp.int32, (part, reach), 1) - lax.broadcasted_iota(
        jnp.int32, (part, reach), 0
    )
    picks = []
    for n in range(places):
        q, r = divmod(n, capacity)
        want = jnp.concatenate([all_ref[q, r : r + 1, :]] * (reach // LANES), axis=1)
        picks.append(jnp.where(skew == want * part, 1.0, 0.0).astype(half))
    gathered = dot(jnp.concatenate(picks, axis=0), vol_half_ref[...].reshape(reach, PIX)).astype(half)
    for n in range(places):
        send_a[n] = gathered[n * part : (n + 1) * part]

    def exchange_copy(phase, d):
        peer = peers[d]
        return angle_copy(
            phase, d,
            sends[phase].at[pl.ds(peer * capacity, capacity)],
            recvs[phase].at[pl.ds(g * capacity, capacity)],
        )

    own = pl.ds(g * capacity, capacity)
    fetches = [exchange_copy(0, d) for d in rising]
    for copy in fetches:
        copy.start()
    recv_a[own] = send_a[own]

    lax.fori_loop(1, rows_ref.shape[1] // CHUNK, step, 0)

    rims = [[], []]
    grads = []
    for channel in (1, 0):
        for side in range(2):
            rim_ref[0, channel, :, lanes[side]] = acc_ref[channel, side, HALO + band :].astype(half)
            rim_ref[1, channel, :, lanes[side]] = acc_ref[channel, side, :HALO].astype(half)
        for way in range(2):
            where = {"tile": below if way == 0 else upper}
            other = dict(where, half=1 - h)
            index = 6 + way * 5 + channel * 2
            pair_of = [
                near(index, rim_ref.at[way, channel, away, :], rim_here_ref.at[way, h, channel], other),
                near(index + 1, rim_ref.at[way, channel, here, :], rim_here_ref.at[way, h, channel], where),
            ]
            rims[way].append(pair_of)

            def send(copies=pair_of):
                for copy in copies:
                    copy.start()

            when_sent(way, send)
        for side in range(2):
            grad_ref[channel, :, lanes[side]] = acc_ref[channel, side, HALO : HALO + band]
        grads.append(
            near(4 + channel, grad_ref.at[channel, away, :], both_grad_ref.at[h, channel], {"half": 1 - h})
        )
        grads[-1].start()
    for way in range(2):
        where = {"tile": below if way == 0 else upper}
        rims[way].append([near(10 + way * 5, rim_ref.at[way, :, away, :], rim_away_ref.at[way], where)])
        when_sent(way, rims[way][-1][0].start)
    both_grad_ref[h] = grad_ref[:, here, :]
    tile_copy.wait_recv()
    beside = near(16, far_tile_ref.at[h, column], far_tile_ref.at[h, column], {"tile": t + 1 - 2 * column})
    beside.start()

    for copy in fetches:
        copy.wait_recv()

    def projected(phase, pair):
        total = jnp.zeros((part, RB), jnp.float32)
        for c in range(per_block):
            slot = pair * per_block + c
            picked = recvs[phase][place_ref[slot]]
            total = total + live_ref[slot] * lax.dot_general(
                picked, weight_ref[slot], (((1,), (1,)), ((), ())),
                preferred_element_type=jnp.float32,
            )
        return total

    sinos = [projected(0, pair) for pair in range(pairs)]

    def received(stage):
        for way in range(2):
            def take(copies=rims[way][stage]):
                for copy in copies:
                    copy.wait_recv()

            when_received(way, take)

    def renewed(angle, channel):
        around = both_grad_ref[angle, channel] + rim_here_ref[0, angle, channel].astype(jnp.float32)
        around = around + rim_here_ref[1, angle, channel].astype(jnp.float32)
        return both_base_ref[angle, channel] - descent * around

    base_copy.wait_recv()
    mult_copy.wait_recv()
    grads[0].wait_recv()
    received(0)
    news = [renewed(angle, 1) for angle in range(angles)]
    for pair in range(pairs):
        angle, k = divmod(pair, NRB)
        rays = slice(k * RB, (k + 1) * RB)
        target = news[angle][:, rays] + both_mult_ref[angle, 1, :, rays] / penalty
        residual_ref[pair] = (sinos[pair] - target).astype(half)

    def spread(n):
        slot = slot_ref[n]
        term = dot(residual_ref[lax.div(slot, per_block)], weight_ref[slot])
        return (used_ref[n] * term).astype(half)

    for r in range(capacity):
        n = twin * capacity + r
        twin_send_ref[r] = residual_ref[lax.div(slot_ref[n], per_block)] * used_ref[n].astype(half)
    terms = [angle_copy(1, across, twin_send_ref, twin_recv_ref)]
    terms[0].start()
    for d in paired:
        if d == across:
            continue
        peer = peers[d]
        for r in range(capacity):
            send_b[peer * capacity + r] = spread(peer * capacity + r)
        terms.append(exchange_copy(1, d))
        terms[-1].start()
    for r in range(capacity):
        recv_b[g * capacity + r] = spread(g * capacity + r)

    beside.wait_recv()
    inside = near(17, far_tile_ref.at[h], far_tile_ref.at[h], {"half": 1 - h})
    inside.start()

    width = places * part
    per_tile = LANES // part
    tile_lane = lax.broadcasted_iota(jnp.int32, (1, LANES), 1)
    keys = []
    for first in range(0, places, per_tile):
        key = jnp.zeros((1, LANES), jnp.int32)
        for n in range(first, first + per_tile):
            q, r = divmod(n, capacity)
            key = jnp.where(tile_lane // part == n - first, all_ref[q, r : r + 1, :], key)
        keys.append(key * part + tile_lane % part)
    key = jnp.concatenate(keys, axis=1)
    merge_ref[...] = jnp.where(
        lax.broadcasted_iota(jnp.int32, (reach, width), 0) == key, 1.0, 0.0
    ).astype(half)

    grads[1].wait_recv()
    received(1)
    received(2)
    for angle in range(angles):
        new_mult_ref[angle, 0] = both_mult_ref[angle, 0] + penalty * (renewed(angle, 0) - 1.0)
    for channel in range(2):
        updated_ref[0, channel, here, :] = renewed(h, channel)
        far = grad_ref[channel, away, :] + rim_away_ref[0, channel].astype(jnp.float32)
        far = far + rim_away_ref[1, channel].astype(jnp.float32)
        updated_ref[0, channel, away, :] = base_ref[channel, away, :] - descent * far
    id_local.wait()
    inside.wait_recv()
    terms[0].wait_recv()
    far_tiles = [
        jnp.concatenate([far_tile_ref[k // 2, k % 2, r] for k in range(4)], axis=0)
        for r in range(capacity)
    ]
    for r in range(capacity):
        recv_b[twin * capacity + r] = dot(twin_recv_ref[r], far_tiles[r]).astype(half)
    for copy in terms[1:]:
        copy.wait_recv()
    total = dot(merge_ref[...], recv_b[...].reshape(width, PIX)).reshape(own_blocks, part, PIX)
    block = vol_ref[...]
    new_vol = block - volume_step * (total + damping * block)
    new_vol_ref[...] = new_vol
    vol_half_ref[...] = new_vol.astype(half)
    for r in range(capacity):
        part_send_ref[r] = lax.dot_general(
            vol_half_ref[all_smem[twin, r, 0]], far_tiles[r], (((1,), (1,)), ((), ())),
            preferred_element_type=jnp.float32,
        ).astype(half)
    renewals = [angle_copy(2, across, part_send_ref, part_recv_ref)]
    renewals[0].start()
    for d in paired:
        if d == across:
            continue
        peer = peers[d]
        for r in range(capacity):
            send_c[peer * capacity + r] = vol_half_ref[all_smem[peer, r, 0]]
        renewals.append(exchange_copy(2, d))
        renewals[-1].start()
    for r in range(capacity):
        recv_c[g * capacity + r] = vol_half_ref[all_smem[g, r, 0]]
    for copy in renewals:
        copy.wait_recv()
    for pair in range(pairs):
        angle, k = divmod(pair, NRB)
        rays = slice(k * RB, (k + 1) * RB)
        fresh = projected(2, pair)
        for r in range(capacity):
            n = twin * capacity + r
            mine = jnp.where(lax.div(slot_ref[n], per_block) == pair, used_ref[n], 0.0)
            fresh = fresh + mine * part_recv_ref[r].astype(jnp.float32)
        new_mult_ref[angle, 1, :, rays] = both_mult_ref[angle, 1, :, rays] + penalty * (
            news[angle][:, rays] - fresh
        )
    for copy in id_copies + fetches + terms + renewals + grads + [base_copy, mult_copy, tile_copy, beside, inside]:
        copy.wait_send()
    for way in range(2):
        def settle(copies=sum(rims[way], [halo[way]])):
            for copy in copies:
                copy.wait_send()

        when_sent(way, settle)


def admm_step(ray_blocks, counts, rows, cols, own, multiplier, prior, measured, field, mask, volume, weights):
    groups = lax.axis_size("angle")
    tiles = lax.axis_size("tile")
    slots = ray_blocks.size
    capacity = max(2, -(-slots // groups))
    places = groups * capacity
    left_f, right_f = dft_blocks(-1.0)
    left_b, right_b = dft_blocks(1.0)
    left_f, left_b = (split_table(m) for m in (left_f, left_b))
    tables = [left_f, jnp.asarray(right_f, jnp.bfloat16), left_b, jnp.asarray(right_b, jnp.bfloat16)]
    vmem = pl.BlockSpec(memory_space=pltpu.VMEM)
    band = own.shape[2]
    part = band // 2
    assert band == HALO and capacity <= ROWS and groups & (groups - 1) == 0 and tiles % 2 == 0
    ext_rows = band + 2 * HALO
    own_blocks = volume.shape[0]
    block = volume.shape[1:]
    weights = weights.reshape((slots,) + weights.shape[3:])
    f32 = jnp.float32
    half = jnp.bfloat16
    operands = [
        ray_blocks, counts, rows, cols, own, multiplier, prior, field, mask, *tables,
        measured, volume, weights,
    ]
    spaces = [pltpu.SMEM] * 4 + [pltpu.VMEM] * 12
    return pl.pallas_call(
        functools.partial(step_kernel, groups, tiles, capacity),
        out_shape=(
            jax.ShapeDtypeStruct(own.shape, f32),
            jax.ShapeDtypeStruct(volume.shape, f32),
            jax.ShapeDtypeStruct((2, 2, part, NW), f32),
        ),
        in_specs=[pl.BlockSpec(memory_space=pltpu.HBM)] * 16,
        out_specs=(vmem, vmem, vmem),
        scratch_shapes=[
            *[space(x.shape, x.dtype) for space, x in zip(spaces, operands)],
            pltpu.SMEM((groups, ROWS, LANES), jnp.int32),
            pltpu.SMEM((slots,), jnp.int32),
            pltpu.SMEM((slots,), jnp.int32),
            pltpu.SMEM((places,), jnp.int32),
            pltpu.SMEM((places,), f32),
            pltpu.SMEM((slots,), f32),
            pltpu.VMEM((groups, ROWS, LANES), jnp.int32),
            pltpu.VMEM((groups, ROWS, LANES), jnp.int32),
            pltpu.VMEM((2, HALO, NW), half),
            pltpu.VMEM((2, HALO, NW), half),
            pltpu.VMEM((2, HALO, NW), half),
            pltpu.VMEM((2, NW // PC, ext_rows, PC), f32),
            pltpu.VMEM((2, NW // PC, ext_rows, PC), f32),
            pltpu.VMEM((2, PR, PC), f32),
            pltpu.VMEM((CHUNK, 2, 2 * (ext_rows - PR) + PR, PC), f32),
            pltpu.VMEM((2, band, NW), f32),
            pltpu.VMEM((2, band, NW), f32),
            *[pltpu.VMEM((2, 2, part, NW), f32)] * 3,
            pltpu.VMEM((2, 2, HALO, NW), half),
            pltpu.VMEM((2, 2, 2, part, NW), half),
            pltpu.VMEM((2, 2, part, NW), half),
            pltpu.VMEM((own_blocks,) + block, half),
            pltpu.VMEM((own_blocks * part, places * part), half),
            pltpu.VMEM((slots // weights_per_block(ray_blocks), part, RB), half),
            pltpu.VMEM((capacity, RB // 4, PIX), half),
            pltpu.VMEM((2, 2, capacity, RB // 4, PIX), half),
            *[pltpu.VMEM((capacity, part, RB), half)] * 4,
            *[pltpu.VMEM((places,) + block, half)] * 6,
            pltpu.SemaphoreType.DMA((5, groups)),
            pltpu.SemaphoreType.DMA((5, groups)),
            pltpu.SemaphoreType.DMA((18,)),
            pltpu.SemaphoreType.DMA((18,)),
            pltpu.SemaphoreType.DMA((17,)),
        ],
        compiler_params=pltpu.CompilerParams(
            collective_id=1, has_side_effects=True, vmem_limit_bytes=32 * 1024 * 1024
        ),
    )(*[pltpu.with_memory_space_constraint(x, pltpu.HBM) for x in operands])


def weights_per_block(ray_blocks):
    return ray_blocks.shape[2]


def write_kernel(a_ref, b_ref, c_ref, a_out, b_out, c_out, sems):
    copies = [
        pltpu.make_async_copy(source, target, sems.at[i])
        for i, (source, target) in enumerate(((a_ref, a_out), (b_ref, b_out), (c_ref, c_out)))
    ]
    for copy in copies:
        copy.start()
    for copy in copies:
        copy.wait()


def write_out(values):
    return pl.pallas_call(
        write_kernel,
        out_shape=tuple(jax.ShapeDtypeStruct(v.shape, v.dtype) for v in values),
        in_specs=[pl.BlockSpec(memory_space=pltpu.VMEM)] * 3,
        out_specs=tuple([pl.BlockSpec(memory_space=pl.ANY)] * 3),
        scratch_shapes=[pltpu.SemaphoreType.DMA((3,))],
        compiler_params=pltpu.CompilerParams(vmem_limit_bytes=8 * 1024 * 1024),
    )(*values)


def shards(
    projection,
    multiplier,
    reprojection,
    intensity,
    row_start,
    column_start,
    probe_field,
    probe_mask,
    weights,
    ray_blocks,
    ray_counts,
    volume,
):
    return write_out(
        admm_step(
            ray_blocks, ray_counts, row_start, column_start, projection, multiplier, reprojection,
            intensity, probe_field, probe_mask, volume, weights,
        )
    )


def solution(mesh):
    return jax.shard_map(
        shards,
        mesh=mesh,
        in_specs=(
            P(("angle", "half"), None, "tile", None),
            P(("angle", "half"), None, "tile", None),
            P(("angle", "half"), "tile", None),
            P(("angle", "half"), "tile", None, None),
            P(("angle", "half"), "tile"),
            P(("angle", "half"), "tile"),
            P(),
            P(),
            P("angle", None, None, None, None),
            P("angle", None, None),
            P("angle", None),
            P("angle", ("tile", "half"), None),
        ),
        out_specs=(
            P(("angle", "half"), None, "tile", None),
            P("angle", ("tile", "half"), None),
            P("angle", None, ("tile", "half"), None),
        ),
        check_vma=False,
    )
```

```python
import functools

import jax
import jax.numpy as jnp
import numpy as np
from jax import lax
from jax.experimental import pallas as pl
from jax.experimental.pallas import tpu as pltpu
from jax.sharding import PartitionSpec as P

PR = 64
PC = 128
NW = 256
PIX = 512
RB = 128
CMAX = 4
HALO = 32
NRB = 2


penalty = 0.5
descent = 0.25
volume_step = 1.0
damping = 0.1


def dft_blocks(sign):
    def table(length):
        counter = np.arange(length)
        phase = (counter[:, None] * counter[None, :] % length) * (2.0 * np.pi / length)
        return np.cos(phase) / np.sqrt(length), sign * np.sin(phase) / np.sqrt(length)

    row_cos, row_sin = table(PR)
    col_cos, col_sin = table(PC)
    left = np.block([[row_cos, -row_sin], [row_sin, row_cos]])
    right = np.block([[col_cos, col_sin], [-col_sin, col_cos]])
    return left.astype(np.float32), right.astype(np.float32)


def split_table(matrix):
    coarse = matrix.astype(jnp.bfloat16)
    rest = (matrix - coarse.astype(np.float32)).astype(jnp.bfloat16)
    return jnp.asarray(np.concatenate([coarse, rest], axis=1))


MESH = pl.DeviceIdType.MESH
CHUNK = 16
ROWS = 8
LANES = 128


def orders(groups):
    rising = list(range(1, groups))
    return rising, [groups // 2] + [d for d in reversed(rising) if 2 * d != groups]


def flipped(index, mask, count):
    out = jnp.int32(0)
    bit = 1
    while bit < count:
        out = out + lax.rem(lax.div(index, bit) + mask // bit, 2) * bit
        bit *= 2
    return out


def step_kernel(
    groups, tiles, capacity,
    mine_hbm, counts_hbm, rows_hbm, cols_hbm, proj_hbm, mult_hbm, prior_hbm, field_hbm, mask_hbm,
    left_f_hbm, right_f_hbm, left_b_hbm, right_b_hbm, measured_hbm, vol_hbm, weight_hbm,
    updated_ref, new_vol_ref, new_mult_ref,
    mine_ref, counts_ref, rows_ref, cols_ref, proj_ref, mult_ref, prior_ref, field_ref, mask_ref,
    left_f_ref, right_f_ref, left_b_ref, right_b_ref, measured_ref, vol_ref, weight_ref,
    all_smem, place_ref, inside_ref, slot_ref, used_ref, live_ref,
    ids_ref, all_ref, edge_ref, before_ref, after_ref,
    ext_ref, acc_ref, wave_ref, stage_ref,
    base_ref, grad_ref, both_base_ref, both_mult_ref, both_grad_ref,
    rim_ref, rim_here_ref, rim_away_ref,
    vol_half_ref, merge_ref, residual_ref,
    tile_ref, far_tile_ref, twin_send_ref, twin_recv_ref, part_send_ref, part_recv_ref,
    send_a, send_b, send_c, recv_a, recv_b, recv_c,
    send_sem, recv_sem, near_send, near_recv, local_sem,
):
    g = lax.axis_index("angle")
    t = lax.axis_index("tile")
    h = lax.axis_index("half")
    band = proj_ref.shape[2]
    part = band // 2
    places = groups * capacity
    own_blocks = vol_ref.shape[0]
    angles, blocks, per_block = mine_ref.shape
    slots = angles * blocks * per_block
    pairs = slots // per_block
    has_up = t > 0
    has_down = t < tiles - 1
    half = jnp.bfloat16
    sends = (send_a, send_b, send_c)
    recvs = (recv_a, recv_b, recv_c)
    lanes = [slice(0, PC), slice(PC, NW)]
    rising, paired = orders(groups)
    peers = {m: flipped(g, m, groups) for m in rising}
    across = groups // 2
    twin = lax.rem(g + across, groups)
    column = lax.rem(t, 2)
    quarter = RB // 4

    def where_of(slot):
        pair, c = divmod(slot, per_block)
        angle, block = divmod(pair, blocks)
        return angle, block, c

    barrier = pltpu.get_barrier_semaphore()

    def greet(where):
        pl.semaphore_signal(barrier, inc=1, device_id=where, device_id_type=MESH)

    for d in rising:
        greet({"angle": peers[d]})
    greet({"half": 1 - h})

    @pl.when(has_up)
    def _():
        greet({"tile": t - 1})
        greet({"tile": t - 1, "half": 1 - h})

    @pl.when(has_down)
    def _():
        greet({"tile": t + 1})
        greet({"tile": t + 1, "half": 1 - h})

    sources = (
        mine_hbm, counts_hbm, rows_hbm, cols_hbm, proj_hbm, mult_hbm, prior_hbm, field_hbm, mask_hbm,
        left_f_hbm, right_f_hbm, left_b_hbm, right_b_hbm, measured_hbm, vol_hbm, weight_hbm,
    )
    targets = (
        mine_ref, counts_ref, rows_ref, cols_ref, proj_ref, mult_ref, prior_ref, field_ref, mask_ref,
        left_f_ref, right_f_ref, left_b_ref, right_b_ref, measured_ref, vol_ref, weight_ref,
    )
    loads = [
        pltpu.make_async_copy(source, target, local_sem.at[i])
        for i, (source, target) in enumerate(zip(sources, targets))
    ]
    for load in loads:
        load.start()

    @pl.when(jnp.logical_not(has_up))
    def _():
        before_ref[...] = jnp.zeros_like(before_ref)
        rim_here_ref[0] = jnp.zeros(rim_here_ref.shape[1:], half)
        rim_away_ref[0] = jnp.zeros(rim_away_ref.shape[1:], half)

    @pl.when(jnp.logical_not(has_down))
    def _():
        after_ref[...] = jnp.zeros_like(after_ref)
        rim_here_ref[1] = jnp.zeros(rim_here_ref.shape[1:], half)
        rim_away_ref[1] = jnp.zeros(rim_away_ref.shape[1:], half)

    acc_ref[...] = jnp.zeros_like(acc_ref)
    stage_ref[...] = jnp.zeros_like(stage_ref)
    ids_ref[...] = jnp.zeros_like(ids_ref)

    for load in loads[:2]:
        load.wait()
    blocks_of = [mine_ref[where_of(s)] for s in range(slots)]
    owners = [lax.div(b, own_blocks) for b in blocks_of]
    for s in range(slots):
        rank = jnp.int32(0)
        for earlier in range(s):
            rank = rank + jnp.where(owners[earlier] == owners[s], 1, 0)
        place_ref[s] = owners[s] * capacity + rank
        inside_ref[s] = lax.rem(blocks_of[s], own_blocks)
        angle, block, c = where_of(s)
        live_ref[s] = jnp.where(c < counts_ref[angle, block], 1.0, 0.0)

    def slot_of(n, carry):
        slot = jnp.int32(0)
        used = jnp.float32(0.0)
        for s in range(slots):
            hit = place_ref[s] == n
            slot = jnp.where(hit, s, slot)
            used = jnp.where(hit, live_ref[s], used)
        slot_ref[n] = slot
        used_ref[n] = used
        return carry

    lax.fori_loop(0, places, slot_of, 0)
    for n in range(places):
        q, r = divmod(n, capacity)
        ids_ref[q, r : r + 1, :] = jnp.full((1, LANES), inside_ref[slot_ref[n]], jnp.int32)

    away = pl.ds(pl.multiple_of((1 - h) * part, part), part)
    here = pl.ds(pl.multiple_of(h * part, part), part)
    for load in loads[4:9]:
        load.wait()
    edge_ref[...] = proj_ref[0].astype(half)
    for channel in range(2):
        old = proj_ref[0, channel]
        held = 1.0 if channel == 0 else prior_ref[0]
        base_ref[channel] = old - descent * (penalty * (old - held) + mult_ref[0, channel])
    for side in range(2):
        ext_ref[:, side, HALO : HALO + band] = proj_ref[0, :, :, lanes[side]]
    mask = mask_ref[...].astype(jnp.float32)
    wave_ref[0] = field_ref[0] * mask
    wave_ref[1] = field_ref[1] * mask
    both_base_ref[h] = base_ref[:, here, :]
    both_mult_ref[h] = mult_ref[0, :, here, :]
    pl.semaphore_wait(
        barrier, groups + 2 * has_up.astype(jnp.int32) + 2 * has_down.astype(jnp.int32)
    )

    def angle_copy(phase, d, source, target):
        return pltpu.make_async_remote_copy(
            src_ref=source,
            dst_ref=target,
            send_sem=send_sem.at[phase, d],
            recv_sem=recv_sem.at[phase, d],
            device_id={"angle": peers[d]},
            device_id_type=MESH,
        )

    def near(index, source, target, where):
        return pltpu.make_async_remote_copy(
            src_ref=source,
            dst_ref=target,
            send_sem=near_send.at[index],
            recv_sem=near_recv.at[index],
            device_id=where,
            device_id_type=MESH,
        )

    below = jnp.minimum(t + 1, tiles - 1)
    upper = jnp.maximum(t - 1, 0)

    def when_sent(way, act):
        pl.when(has_down if way == 0 else has_up)(act)

    def when_received(way, act):
        pl.when(has_up if way == 0 else has_down)(act)

    id_copies = [
        angle_copy(3, d, ids_ref.at[peers[d]], all_ref.at[g]) for d in rising
    ]
    for copy in id_copies:
        copy.start()
    halo = [
        near(0, edge_ref, before_ref, {"tile": below}),
        near(1, edge_ref, after_ref, {"tile": upper}),
    ]
    for way in range(2):
        when_sent(way, halo[way].start)
    base_copy = near(2, base_ref.at[:, away, :], both_base_ref.at[h], {"half": 1 - h})
    mult_copy = near(3, mult_ref.at[0, :, away, :], both_mult_ref.at[h], {"half": 1 - h})
    base_copy.start()
    mult_copy.start()
    loads[14].wait()
    vol_half_ref[...] = vol_ref[...].astype(half)
    loads[15].wait()
    first_ray = pl.multiple_of((2 * h + column) * quarter, quarter)
    for r in range(capacity):
        tile_ref[r] = weight_ref[slot_ref[twin * capacity + r], pl.ds(first_ray, quarter), :]
        recv_c[twin * capacity + r] = jnp.zeros(recv_c.shape[1:], half)

    tile_copy = angle_copy(4, across, tile_ref, far_tile_ref.at[h, column])
    tile_copy.start()
    all_ref[g] = ids_ref[g]
    for load in loads[2:4] + loads[9:14]:
        load.wait()
    for way in range(2):
        when_received(way, halo[way].wait_recv)
    for side in range(2):
        ext_ref[:, side, :HALO] = before_ref[:, :, lanes[side]].astype(jnp.float32)
        ext_ref[:, side, HALO + band :] = after_ref[:, :, lanes[side]].astype(jnp.float32)

    lane = lax.broadcasted_iota(jnp.int32, (PR, PC), 1)
    ext_rows = band + 2 * HALO
    wide_lane = lax.broadcasted_iota(jnp.int32, (ext_rows, PC), 1)

    def dot(a, b):
        return jnp.dot(a, b, preferred_element_type=jnp.float32)

    def step(chunk, carry):
        waves = []
        spots = []
        for j in range(CHUNK):
            p = chunk * CHUNK + j
            row = rows_ref[0, p] + HALO
            col = cols_ref[0, p]
            spots.append((row, col))
            back_shift = lax.rem(NW - col, PC)

            def window(channel):
                near = pltpu.roll(ext_ref[channel, 0, pl.ds(row, PR), :], back_shift, 1)
                next_ = pltpu.roll(ext_ref[channel, 1, pl.ds(row, PR), :], back_shift, 1)
                return jnp.where(lane + col < PC, near, next_)

            o_re = window(0)
            o_im = window(1)
            p_re, p_im = wave_ref[0], wave_ref[1]
            waves.append(
                jnp.concatenate([p_re * o_re - p_im * o_im, p_re * o_im + p_im * o_re], axis=0)
            )
        wide = jnp.concatenate(waves, axis=1).astype(half)
        first = dot(left_f_ref[...], jnp.concatenate([wide, wide], axis=0)).astype(half)
        tall = jnp.concatenate(
            [
                jnp.concatenate(
                    [first[:PR, j * PC : (j + 1) * PC], first[PR:, j * PC : (j + 1) * PC]], axis=1
                )
                for j in range(CHUNK)
            ],
            axis=0,
        )
        far = dot(tall, right_f_ref[...])
        f_re, f_im = far[:, :PC], far[:, PC:]
        measured = measured_ref[0, pl.ds(chunk * CHUNK, CHUNK)].astype(jnp.float32)
        measured = measured.reshape(CHUNK * PR, PC)
        factor = 1.0 - jnp.sqrt(measured) * lax.rsqrt(f_re * f_re + f_im * f_im + 1.0)
        scaled = jnp.concatenate([f_re * factor, f_im * factor], axis=1).astype(half)
        second = dot(scaled, right_b_ref[...]).astype(half)
        wide = jnp.concatenate(
            [
                jnp.concatenate(
                    [second[j * PR : (j + 1) * PR, :PC], second[j * PR : (j + 1) * PR, PC:]], axis=0
                )
                for j in range(CHUNK)
            ],
            axis=1,
        )
        back = dot(left_b_ref[...], jnp.concatenate([wide, wide], axis=0))
        above = ext_rows - PR
        for j in range(CHUNK):
            shift = lax.rem(spots[j][1], PC)
            b_re = back[:PR, j * PC : (j + 1) * PC]
            b_im = back[PR:, j * PC : (j + 1) * PC]
            p_re, p_im = wave_ref[0], wave_ref[1]
            stage_ref[j, 0, above : above + PR] = pltpu.roll(p_re * b_re + p_im * b_im, shift, 1)
            stage_ref[j, 1, above : above + PR] = pltpu.roll(p_re * b_im - p_im * b_re, shift, 1)
        for channel in range(2):
            first_half = acc_ref[channel, 0]
            next_half = acc_ref[channel, 1]
            for j in range(CHUNK):
                row, col = spots[j]
                values = stage_ref[j, channel, pl.ds(above - row, ext_rows), :]
                first_half = first_half + jnp.where(wide_lane >= col, values, 0.0)
                next_half = next_half + jnp.where(wide_lane >= col, 0.0, values)
            acc_ref[channel, 0] = first_half
            acc_ref[channel, 1] = next_half
        return carry

    lax.fori_loop(0, 1, step, 0)

    for copy in id_copies:
        copy.wait_recv()
    id_local = pltpu.make_async_copy(all_ref, all_smem, local_sem.at[len(loads)])
    id_local.start()
    reach = own_blocks * part
    skew = lax.broadcasted_iota(jnp.int32, (part, reach), 1) - lax.broadcasted_iota(
        jnp.int32, (part, reach), 0
    )
    picks = []
    for n in range(places):
        q, r = divmod(n, capacity)
        want = jnp.concatenate([all_ref[q, r : r + 1, :]] * (reach // LANES), axis=1)
        picks.append(jnp.where(skew == want * part, 1.0, 0.0).astype(half))
    gathered = dot(jnp.concatenate(picks, axis=0), vol_half_ref[...].reshape(reach, PIX)).astype(half)
    for n in range(places):
        send_a[n] = gathered[n * part : (n + 1) * part]

    def exchange_copy(phase, d):
        peer = peers[d]
        return angle_copy(
            phase, d,
            sends[phase].at[pl.ds(peer * capacity, capacity)],
            recvs[phase].at[pl.ds(g * capacity, capacity)],
        )

    own = pl.ds(g * capacity, capacity)
    fetches = [exchange_copy(0, d) for d in rising]
    for copy in fetches:
        copy.start()
    recv_a[own] = send_a[own]

    lax.fori_loop(1, rows_ref.shape[1] // CHUNK, step, 0)

    rims = [[], []]
    grads = []
    for channel in (1, 0):
        for side in range(2):
            rim_ref[0, channel, :, lanes[side]] = acc_ref[channel, side, HALO + band :].astype(half)
            rim_ref[1, channel, :, lanes[side]] = acc_ref[channel, side, :HALO].astype(half)
        for way in range(2):
            where = {"tile": below if way == 0 else upper}
            other = dict(where, half=1 - h)
            index = 6 + way * 5 + channel * 2
            pair_of = [
                near(index, rim_ref.at[way, channel, away, :], rim_here_ref.at[way, h, channel], other),
                near(index + 1, rim_ref.at[way, channel, here, :], rim_here_ref.at[way, h, channel], where),
            ]
            rims[way].append(pair_of)

            def send(copies=pair_of):
                for copy in copies:
                    copy.start()

            when_sent(way, send)
        for side in range(2):
            grad_ref[channel, :, lanes[side]] = acc_ref[channel, side, HALO : HALO + band]
        grads.append(
            near(4 + channel, grad_ref.at[channel, away, :], both_grad_ref.at[h, channel], {"half": 1 - h})
        )
        grads[-1].start()
    for way in range(2):
        where = {"tile": below if way == 0 else upper}
        rims[way].append([near(10 + way * 5, rim_ref.at[way, :, away, :], rim_away_ref.at[way], where)])
        when_sent(way, rims[way][-1][0].start)
    both_grad_ref[h] = grad_ref[:, here, :]
    tile_copy.wait_recv()
    beside = near(16, far_tile_ref.at[h, column], far_tile_ref.at[h, column], {"tile": t + 1 - 2 * column})
    beside.start()

    for copy in fetches:
        copy.wait_recv()

    def projected(phase, pair):
        total = jnp.zeros((part, RB), jnp.float32)
        for c in range(per_block):
            slot = pair * per_block + c
            picked = recvs[phase][place_ref[slot]]
            total = total + live_ref[slot] * lax.dot_general(
                picked, weight_ref[slot], (((1,), (1,)), ((), ())),
                preferred_element_type=jnp.float32,
            )
        return total

    sinos = [projected(0, pair) for pair in range(pairs)]

    def received(stage):
        for way in range(2):
            def take(copies=rims[way][stage]):
                for copy in copies:
                    copy.wait_recv()

            when_received(way, take)

    def renewed(angle, channel):
        around = both_grad_ref[angle, channel] + rim_here_ref[0, angle, channel].astype(jnp.float32)
        around = around + rim_here_ref[1, angle, channel].astype(jnp.float32)
        return both_base_ref[angle, channel] - descent * around

    base_copy.wait_recv()
    mult_copy.wait_recv()
    grads[0].wait_recv()
    received(0)
    news = [renewed(angle, 1) for angle in range(angles)]
    for pair in range(pairs):
        angle, k = divmod(pair, NRB)
        rays = slice(k * RB, (k + 1) * RB)
        target = news[angle][:, rays] + both_mult_ref[angle, 1, :, rays] / penalty
        residual_ref[pair] = (sinos[pair] - target).astype(half)

    def spread(n):
        slot = slot_ref[n]
        term = dot(residual_ref[lax.div(slot, per_block)], weight_ref[slot])
        return (used_ref[n] * term).astype(half)

    for r in range(capacity):
        n = twin * capacity + r
        twin_send_ref[r] = residual_ref[lax.div(slot_ref[n], per_block)] * used_ref[n].astype(half)
    terms = [angle_copy(1, across, twin_send_ref, twin_recv_ref)]
    terms[0].start()
    for d in paired:
        if d == across:
            continue
        peer = peers[d]
        for r in range(capacity):
            send_b[peer * capacity + r] = spread(peer * capacity + r)
        terms.append(exchange_copy(1, d))
        terms[-1].start()
    for r in range(capacity):
        recv_b[g * capacity + r] = spread(g * capacity + r)

    beside.wait_recv()
    inside = near(17, far_tile_ref.at[h], far_tile_ref.at[h], {"half": 1 - h})
    inside.start()

    width = places * part
    per_tile = LANES // part
    tile_lane = lax.broadcasted_iota(jnp.int32, (1, LANES), 1)
    keys = []
    for first in range(0, places, per_tile):
        key = jnp.zeros((1, LANES), jnp.int32)
        for n in range(first, first + per_tile):
            q, r = divmod(n, capacity)
            key = jnp.where(tile_lane // part == n - first, all_ref[q, r : r + 1, :], key)
        keys.append(key * part + tile_lane % part)
    key = jnp.concatenate(keys, axis=1)
    merge_ref[...] = jnp.where(
        lax.broadcasted_iota(jnp.int32, (reach, width), 0) == key, 1.0, 0.0
    ).astype(half)

    grads[1].wait_recv()
    received(1)
    received(2)
    for angle in range(angles):
        new_mult_ref[angle, 0] = both_mult_ref[angle, 0] + penalty * (renewed(angle, 0) - 1.0)
    for channel in range(2):
        updated_ref[0, channel, here, :] = renewed(h, channel)
        far = grad_ref[channel, away, :] + rim_away_ref[0, channel].astype(jnp.float32)
        far = far + rim_away_ref[1, channel].astype(jnp.float32)
        updated_ref[0, channel, away, :] = base_ref[channel, away, :] - descent * far
    id_local.wait()
    inside.wait_recv()
    terms[0].wait_recv()
    far_tiles = [
        jnp.concatenate([far_tile_ref[k // 2, k % 2, r] for k in range(4)], axis=0)
        for r in range(capacity)
    ]
    for r in range(capacity):
        recv_b[twin * capacity + r] = dot(twin_recv_ref[r], far_tiles[r]).astype(half)
    for copy in terms[1:]:
        copy.wait_recv()
    total = dot(merge_ref[...], recv_b[...].reshape(width, PIX)).reshape(own_blocks, part, PIX)
    block = vol_ref[...]
    new_vol = block - volume_step * (total + damping * block)
    new_vol_ref[...] = new_vol
    vol_half_ref[...] = new_vol.astype(half)
    for r in range(capacity):
        part_send_ref[r] = lax.dot_general(
            vol_half_ref[all_smem[twin, r, 0]], far_tiles[r], (((1,), (1,)), ((), ())),
            preferred_element_type=jnp.float32,
        ).astype(half)
    renewals = [angle_copy(2, across, part_send_ref, part_recv_ref)]
    renewals[0].start()
    for d in paired:
        if d == across:
            continue
        peer = peers[d]
        for r in range(capacity):
            send_c[peer * capacity + r] = vol_half_ref[all_smem[peer, r, 0]]
        renewals.append(exchange_copy(2, d))
        renewals[-1].start()
    for r in range(capacity):
        recv_c[g * capacity + r] = vol_half_ref[all_smem[g, r, 0]]
    for copy in renewals:
        copy.wait_recv()
    for pair in range(pairs):
        angle, k = divmod(pair, NRB)
        rays = slice(k * RB, (k + 1) * RB)
        fresh = projected(2, pair)
        for r in range(capacity):
            n = twin * capacity + r
            mine = jnp.where(lax.div(slot_ref[n], per_block) == pair, used_ref[n], 0.0)
            fresh = fresh + mine * part_recv_ref[r].astype(jnp.float32)
        new_mult_ref[angle, 1, :, rays] = both_mult_ref[angle, 1, :, rays] + penalty * (
            news[angle][:, rays] - fresh
        )
    for copy in id_copies + fetches + terms + renewals + grads + [base_copy, mult_copy, tile_copy, beside, inside]:
        copy.wait_send()
    for way in range(2):
        def settle(copies=sum(rims[way], [halo[way]])):
            for copy in copies:
                copy.wait_send()

        when_sent(way, settle)


def admm_step(ray_blocks, counts, rows, cols, own, multiplier, prior, measured, field, mask, volume, weights):
    groups = lax.axis_size("angle")
    tiles = lax.axis_size("tile")
    slots = ray_blocks.size
    capacity = max(2, -(-slots // groups))
    places = groups * capacity
    left_f, right_f = dft_blocks(-1.0)
    left_b, right_b = dft_blocks(1.0)
    left_f, left_b = (split_table(m) for m in (left_f, left_b))
    tables = [left_f, jnp.asarray(right_f, jnp.bfloat16), left_b, jnp.asarray(right_b, jnp.bfloat16)]
    vmem = pl.BlockSpec(memory_space=pltpu.VMEM)
    band = own.shape[2]
    part = band // 2
    assert band == HALO and capacity <= ROWS and groups & (groups - 1) == 0 and tiles % 2 == 0
    ext_rows = band + 2 * HALO
    own_blocks = volume.shape[0]
    block = volume.shape[1:]
    weights = weights.reshape((slots,) + weights.shape[3:])
    f32 = jnp.float32
    half = jnp.bfloat16
    operands = [
        ray_blocks, counts, rows, cols, own, multiplier, prior, field, mask, *tables,
        measured, volume, weights,
    ]
    spaces = [pltpu.SMEM] * 4 + [pltpu.VMEM] * 12
    return pl.pallas_call(
        functools.partial(step_kernel, groups, tiles, capacity),
        out_shape=(
            jax.ShapeDtypeStruct(own.shape, f32),
            jax.ShapeDtypeStruct(volume.shape, f32),
            jax.ShapeDtypeStruct((2, 2, part, NW), f32),
        ),
        in_specs=[pl.BlockSpec(memory_space=pltpu.HBM)] * 16,
        out_specs=(vmem, vmem, vmem),
        scratch_shapes=[
            *[space(x.shape, x.dtype) for space, x in zip(spaces, operands)],
            pltpu.SMEM((groups, ROWS, LANES), jnp.int32),
            pltpu.SMEM((slots,), jnp.int32),
            pltpu.SMEM((slots,), jnp.int32),
            pltpu.SMEM((places,), jnp.int32),
            pltpu.SMEM((places,), f32),
            pltpu.SMEM((slots,), f32),
            pltpu.VMEM((groups, ROWS, LANES), jnp.int32),
            pltpu.VMEM((groups, ROWS, LANES), jnp.int32),
            pltpu.VMEM((2, HALO, NW), half),
            pltpu.VMEM((2, HALO, NW), half),
            pltpu.VMEM((2, HALO, NW), half),
            pltpu.VMEM((2, NW // PC, ext_rows, PC), f32),
            pltpu.VMEM((2, NW // PC, ext_rows, PC), f32),
            pltpu.VMEM((2, PR, PC), f32),
            pltpu.VMEM((CHUNK, 2, 2 * (ext_rows - PR) + PR, PC), f32),
            pltpu.VMEM((2, band, NW), f32),
            pltpu.VMEM((2, band, NW), f32),
            *[pltpu.VMEM((2, 2, part, NW), f32)] * 3,
            pltpu.VMEM((2, 2, HALO, NW), half),
            pltpu.VMEM((2, 2, 2, part, NW), half),
            pltpu.VMEM((2, 2, part, NW), half),
            pltpu.VMEM((own_blocks,) + block, half),
            pltpu.VMEM((own_blocks * part, places * part), half),
            pltpu.VMEM((slots // weights_per_block(ray_blocks), part, RB), half),
            pltpu.VMEM((capacity, RB // 4, PIX), half),
            pltpu.VMEM((2, 2, capacity, RB // 4, PIX), half),
            *[pltpu.VMEM((capacity, part, RB), half)] * 4,
            *[pltpu.VMEM((places,) + block, half)] * 6,
            pltpu.SemaphoreType.DMA((5, groups)),
            pltpu.SemaphoreType.DMA((5, groups)),
            pltpu.SemaphoreType.DMA((18,)),
            pltpu.SemaphoreType.DMA((18,)),
            pltpu.SemaphoreType.DMA((17,)),
        ],
        compiler_params=pltpu.CompilerParams(
            collective_id=1, has_side_effects=True, vmem_limit_bytes=32 * 1024 * 1024
        ),
    )(*[pltpu.with_memory_space_constraint(x, pltpu.HBM) for x in operands])


def weights_per_block(ray_blocks):
    return ray_blocks.shape[2]


def write_kernel(a_ref, b_ref, c_ref, a_out, b_out, c_out, sems):
    copies = [
        pltpu.make_async_copy(source, target, sems.at[i])
        for i, (source, target) in enumerate(((a_ref, a_out), (b_ref, b_out), (c_ref, c_out)))
    ]
    for copy in copies:
        copy.start()
    for copy in copies:
        copy.wait()


def write_out(values):
    return pl.pallas_call(
        write_kernel,
        out_shape=tuple(jax.ShapeDtypeStruct(v.shape, v.dtype) for v in values),
        in_specs=[pl.BlockSpec(memory_space=pltpu.VMEM)] * 3,
        out_specs=tuple([pl.BlockSpec(memory_space=pl.ANY)] * 3),
        scratch_shapes=[pltpu.SemaphoreType.DMA((3,))],
        compiler_params=pltpu.CompilerParams(vmem_limit_bytes=8 * 1024 * 1024),
    )(*values)


def shards(
    projection,
    multiplier,
    reprojection,
    intensity,
    row_start,
    column_start,
    probe_field,
    probe_mask,
    weights,
    ray_blocks,
    ray_counts,
    volume,
):
    return write_out(
        admm_step(
            ray_blocks, ray_counts, row_start, column_start, projection, multiplier, reprojection,
            intensity, probe_field, probe_mask, volume, weights,
        )
    )


def solution(mesh):
    return jax.shard_map(
        shards,
        mesh=mesh,
        in_specs=(
            P(("angle", "half"), None, "tile", None),
            P(("angle", "half"), None, "tile", None),
            P(("angle", "half"), "tile", None),
            P(("angle", "half"), "tile", None, None),
            P(("angle", "half"), "tile"),
            P(("angle", "half"), "tile"),
            P(),
            P(),
            P("angle", None, None, None, None),
            P("angle", None, None),
            P("angle", None),
            P("angle", ("tile", "half"), None),
        ),
        out_specs=(
            P(("angle", "half"), None, "tile", None),
            P("angle", ("tile", "half"), None),
            P("angle", None, ("tile", "half"), None),
        ),
        check_vma=False,
    )
```

```python
import functools

import jax
import jax.numpy as jnp
import numpy as np
from jax import lax
from jax.experimental import pallas as pl
from jax.experimental.pallas import tpu as pltpu
from jax.sharding import PartitionSpec as P

PR = 64
PC = 128
NW = 256
PIX = 512
RB = 128
CMAX = 4
HALO = 32
NRB = 2


penalty = 0.5
descent = 0.25
volume_step = 1.0
damping = 0.1


def dft_blocks(sign):
    def table(length):
        counter = np.arange(length)
        phase = (counter[:, None] * counter[None, :] % length) * (2.0 * np.pi / length)
        return np.cos(phase) / np.sqrt(length), sign * np.sin(phase) / np.sqrt(length)

    row_cos, row_sin = table(PR)
    col_cos, col_sin = table(PC)
    left = np.block([[row_cos, -row_sin], [row_sin, row_cos]])
    right = np.block([[col_cos, col_sin], [-col_sin, col_cos]])
    return left.astype(np.float32), right.astype(np.float32)


def split_table(matrix):
    coarse = matrix.astype(jnp.bfloat16)
    rest = (matrix - coarse.astype(np.float32)).astype(jnp.bfloat16)
    return jnp.asarray(np.concatenate([coarse, rest], axis=1))


MESH = pl.DeviceIdType.MESH
CHUNK = 16
ROWS = 8
LANES = 128


def orders(groups):
    rising = list(range(1, groups))
    return rising, [groups // 2] + [d for d in reversed(rising) if 2 * d != groups]


def flipped(index, mask, count):
    out = jnp.int32(0)
    bit = 1
    while bit < count:
        out = out + lax.rem(lax.div(index, bit) + mask // bit, 2) * bit
        bit *= 2
    return out


def step_kernel(
    groups, tiles, capacity,
    mine_hbm, counts_hbm, rows_hbm, cols_hbm, proj_hbm, mult_hbm, prior_hbm, field_hbm, mask_hbm,
    left_f_hbm, right_f_hbm, left_b_hbm, right_b_hbm, measured_hbm, vol_hbm, weight_hbm,
    updated_ref, new_vol_ref, new_mult_ref,
    mine_ref, counts_ref, rows_ref, cols_ref, proj_ref, mult_ref, prior_ref, field_ref, mask_ref,
    left_f_ref, right_f_ref, left_b_ref, right_b_ref, measured_ref, vol_ref, weight_ref,
    all_smem, place_ref, inside_ref, slot_ref, used_ref, live_ref,
    ids_ref, all_ref, edge_ref, before_ref, after_ref,
    ext_ref, acc_ref, wave_ref, stage_ref,
    base_ref, grad_ref, both_base_ref, both_mult_ref, both_grad_ref,
    rim_ref, rim_here_ref, rim_away_ref,
    vol_half_ref, merge_ref, residual_ref,
    tile_ref, far_tile_ref, twin_send_ref, twin_recv_ref, part_send_ref, part_recv_ref,
    send_a, send_b, send_c, recv_a, recv_b, recv_c,
    send_sem, recv_sem, near_send, near_recv, local_sem,
):
    g = lax.axis_index("angle")
    t = lax.axis_index("tile")
    h = lax.axis_index("half")
    band = proj_ref.shape[2]
    part = band // 2
    places = groups * capacity
    own_blocks = vol_ref.shape[0]
    angles, blocks, per_block = mine_ref.shape
    slots = angles * blocks * per_block
    pairs = slots // per_block
    has_up = t > 0
    has_down = t < tiles - 1
    half = jnp.bfloat16
    sends = (send_a, send_b, send_c)
    recvs = (recv_a, recv_b, recv_c)
    lanes = [slice(0, PC), slice(PC, NW)]
    rising, paired = orders(groups)
    peers = {m: flipped(g, m, groups) for m in rising}
    across = groups // 2
    twin = lax.rem(g + across, groups)
    column = lax.rem(t, 2)
    quarter = RB // 4

    def where_of(slot):
        pair, c = divmod(slot, per_block)
        angle, block = divmod(pair, blocks)
        return angle, block, c

    barrier = pltpu.get_barrier_semaphore()

    def greet(where):
        pl.semaphore_signal(barrier, inc=1, device_id=where, device_id_type=MESH)

    for d in rising:
        greet({"angle": peers[d]})
    greet({"half": 1 - h})

    @pl.when(has_up)
    def _():
        greet({"tile": t - 1})
        greet({"tile": t - 1, "half": 1 - h})

    @pl.when(has_down)
    def _():
        greet({"tile": t + 1})
        greet({"tile": t + 1, "half": 1 - h})

    sources = (
        mine_hbm, counts_hbm, rows_hbm, cols_hbm, proj_hbm, mult_hbm, prior_hbm, field_hbm, mask_hbm,
        left_f_hbm, right_f_hbm, left_b_hbm, right_b_hbm, measured_hbm, vol_hbm, weight_hbm,
    )
    targets = (
        mine_ref, counts_ref, rows_ref, cols_ref, proj_ref, mult_ref, prior_ref, field_ref, mask_ref,
        left_f_ref, right_f_ref, left_b_ref, right_b_ref, measured_ref, vol_ref, weight_ref,
    )
    loads = [
        pltpu.make_async_copy(source, target, local_sem.at[i])
        for i, (source, target) in enumerate(zip(sources, targets))
    ]
    for load in loads:
        load.start()

    @pl.when(jnp.logical_not(has_up))
    def _():
        before_ref[...] = jnp.zeros_like(before_ref)
        rim_here_ref[0] = jnp.zeros(rim_here_ref.shape[1:], half)
        rim_away_ref[0] = jnp.zeros(rim_away_ref.shape[1:], half)

    @pl.when(jnp.logical_not(has_down))
    def _():
        after_ref[...] = jnp.zeros_like(after_ref)
        rim_here_ref[1] = jnp.zeros(rim_here_ref.shape[1:], half)
        rim_away_ref[1] = jnp.zeros(rim_away_ref.shape[1:], half)

    acc_ref[...] = jnp.zeros_like(acc_ref)
    stage_ref[...] = jnp.zeros_like(stage_ref)
    ids_ref[...] = jnp.zeros_like(ids_ref)

    for load in loads[:2]:
        load.wait()
    blocks_of = [mine_ref[where_of(s)] for s in range(slots)]
    owners = [lax.div(b, own_blocks) for b in blocks_of]
    for s in range(slots):
        rank = jnp.int32(0)
        for earlier in range(s):
            rank = rank + jnp.where(owners[earlier] == owners[s], 1, 0)
        place_ref[s] = owners[s] * capacity + rank
        inside_ref[s] = lax.rem(blocks_of[s], own_blocks)
        angle, block, c = where_of(s)
        live_ref[s] = jnp.where(c < counts_ref[angle, block], 1.0, 0.0)

    def slot_of(n, carry):
        slot = jnp.int32(0)
        used = jnp.float32(0.0)
        for s in range(slots):
            hit = place_ref[s] == n
            slot = jnp.where(hit, s, slot)
            used = jnp.where(hit, live_ref[s], used)
        slot_ref[n] = slot
        used_ref[n] = used
        return carry

    lax.fori_loop(0, places, slot_of, 0)
    for n in range(places):
        q, r = divmod(n, capacity)
        ids_ref[q, r : r + 1, :] = jnp.full((1, LANES), inside_ref[slot_ref[n]], jnp.int32)

    away = pl.ds(pl.multiple_of((1 - h) * part, part), part)
    here = pl.ds(pl.multiple_of(h * part, part), part)
    for load in loads[4:9]:
        load.wait()
    edge_ref[...] = proj_ref[0].astype(half)
    for channel in range(2):
        old = proj_ref[0, channel]
        held = 1.0 if channel == 0 else prior_ref[0]
        base_ref[channel] = old - descent * (penalty * (old - held) + mult_ref[0, channel])
    for side in range(2):
        ext_ref[:, side, HALO : HALO + band] = proj_ref[0, :, :, lanes[side]]
    mask = mask_ref[...].astype(jnp.float32)
    wave_ref[0] = field_ref[0] * mask
    wave_ref[1] = field_ref[1] * mask
    both_base_ref[h] = base_ref[:, here, :]
    both_mult_ref[h] = mult_ref[0, :, here, :]
    pl.semaphore_wait(
        barrier, groups + 2 * has_up.astype(jnp.int32) + 2 * has_down.astype(jnp.int32)
    )

    def angle_copy(phase, d, source, target):
        return pltpu.make_async_remote_copy(
            src_ref=source,
            dst_ref=target,
            send_sem=send_sem.at[phase, d],
            recv_sem=recv_sem.at[phase, d],
            device_id={"angle": peers[d]},
            device_id_type=MESH,
        )

    def near(index, source, target, where):
        return pltpu.make_async_remote_copy(
            src_ref=source,
            dst_ref=target,
            send_sem=near_send.at[index],
            recv_sem=near_recv.at[index],
            device_id=where,
            device_id_type=MESH,
        )

    below = jnp.minimum(t + 1, tiles - 1)
    upper = jnp.maximum(t - 1, 0)

    def when_sent(way, act):
        pl.when(has_down if way == 0 else has_up)(act)

    def when_received(way, act):
        pl.when(has_up if way == 0 else has_down)(act)

    id_copies = [
        angle_copy(3, d, ids_ref.at[peers[d]], all_ref.at[g]) for d in rising
    ]
    for copy in id_copies:
        copy.start()
    halo = [
        near(0, edge_ref, before_ref, {"tile": below}),
        near(1, edge_ref, after_ref, {"tile": upper}),
    ]
    for way in range(2):
        when_sent(way, halo[way].start)
    base_copy = near(2, base_ref.at[:, away, :], both_base_ref.at[h], {"half": 1 - h})
    mult_copy = near(3, mult_ref.at[0, :, away, :], both_mult_ref.at[h], {"half": 1 - h})
    base_copy.start()
    mult_copy.start()
    loads[14].wait()
    vol_half_ref[...] = vol_ref[...].astype(half)
    loads[15].wait()
    first_ray = pl.multiple_of((2 * h + column) * quarter, quarter)
    for r in range(capacity):
        tile_ref[r] = weight_ref[slot_ref[twin * capacity + r], pl.ds(first_ray, quarter), :]

    tile_copy = angle_copy(4, across, tile_ref, far_tile_ref.at[h, column])
    tile_copy.start()
    all_ref[g] = ids_ref[g]
    for load in loads[2:4] + loads[9:14]:
        load.wait()
    for way in range(2):
        when_received(way, halo[way].wait_recv)
    for side in range(2):
        ext_ref[:, side, :HALO] = before_ref[:, :, lanes[side]].astype(jnp.float32)
        ext_ref[:, side, HALO + band :] = after_ref[:, :, lanes[side]].astype(jnp.float32)

    lane = lax.broadcasted_iota(jnp.int32, (PR, PC), 1)
    ext_rows = band + 2 * HALO
    wide_lane = lax.broadcasted_iota(jnp.int32, (ext_rows, PC), 1)

    def dot(a, b):
        return jnp.dot(a, b, preferred_element_type=jnp.float32)

    def step(chunk, carry):
        waves = []
        spots = []
        for j in range(CHUNK):
            p = chunk * CHUNK + j
            row = rows_ref[0, p] + HALO
            col = cols_ref[0, p]
            spots.append((row, col))
            back_shift = lax.rem(NW - col, PC)

            def window(channel):
                near = pltpu.roll(ext_ref[channel, 0, pl.ds(row, PR), :], back_shift, 1)
                next_ = pltpu.roll(ext_ref[channel, 1, pl.ds(row, PR), :], back_shift, 1)
                return jnp.where(lane + col < PC, near, next_)

            o_re = window(0)
            o_im = window(1)
            p_re, p_im = wave_ref[0], wave_ref[1]
            waves.append(
                jnp.concatenate([p_re * o_re - p_im * o_im, p_re * o_im + p_im * o_re], axis=0)
            )
        wide = jnp.concatenate(waves, axis=1).astype(half)
        first = dot(left_f_ref[...], jnp.concatenate([wide, wide], axis=0)).astype(half)
        tall = jnp.concatenate(
            [
                jnp.concatenate(
                    [first[:PR, j * PC : (j + 1) * PC], first[PR:, j * PC : (j + 1) * PC]], axis=1
                )
                for j in range(CHUNK)
            ],
            axis=0,
        )
        far = dot(tall, right_f_ref[...])
        f_re, f_im = far[:, :PC], far[:, PC:]
        measured = measured_ref[0, pl.ds(chunk * CHUNK, CHUNK)].astype(jnp.float32)
        measured = measured.reshape(CHUNK * PR, PC)
        factor = 1.0 - jnp.sqrt(measured) * lax.rsqrt(f_re * f_re + f_im * f_im + 1.0)
        scaled = jnp.concatenate([f_re * factor, f_im * factor], axis=1).astype(half)
        second = dot(scaled, right_b_ref[...]).astype(half)
        wide = jnp.concatenate(
            [
                jnp.concatenate(
                    [second[j * PR : (j + 1) * PR, :PC], second[j * PR : (j + 1) * PR, PC:]], axis=0
                )
                for j in range(CHUNK)
            ],
            axis=1,
        )
        back = dot(left_b_ref[...], jnp.concatenate([wide, wide], axis=0))
        above = ext_rows - PR
        for j in range(CHUNK):
            shift = lax.rem(spots[j][1], PC)
            b_re = back[:PR, j * PC : (j + 1) * PC]
            b_im = back[PR:, j * PC : (j + 1) * PC]
            p_re, p_im = wave_ref[0], wave_ref[1]
            stage_ref[j, 0, above : above + PR] = pltpu.roll(p_re * b_re + p_im * b_im, shift, 1)
            stage_ref[j, 1, above : above + PR] = pltpu.roll(p_re * b_im - p_im * b_re, shift, 1)
        for channel in range(2):
            first_half = acc_ref[channel, 0]
            next_half = acc_ref[channel, 1]
            for j in range(CHUNK):
                row, col = spots[j]
                values = stage_ref[j, channel, pl.ds(above - row, ext_rows), :]
                first_half = first_half + jnp.where(wide_lane >= col, values, 0.0)
                next_half = next_half + jnp.where(wide_lane >= col, 0.0, values)
            acc_ref[channel, 0] = first_half
            acc_ref[channel, 1] = next_half
        return carry

    lax.fori_loop(0, 1, step, 0)

    for copy in id_copies:
        copy.wait_recv()
    id_local = pltpu.make_async_copy(all_ref, all_smem, local_sem.at[len(loads)])
    id_local.start()
    reach = own_blocks * part
    skew = lax.broadcasted_iota(jnp.int32, (part, reach), 1) - lax.broadcasted_iota(
        jnp.int32, (part, reach), 0
    )
    picks = []
    for n in range(places):
        q, r = divmod(n, capacity)
        want = jnp.concatenate([all_ref[q, r : r + 1, :]] * (reach // LANES), axis=1)
        picks.append(jnp.where(skew == want * part, 1.0, 0.0).astype(half))
    gathered = dot(jnp.concatenate(picks, axis=0), vol_half_ref[...].reshape(reach, PIX)).astype(half)
    for n in range(places):
        send_a[n] = gathered[n * part : (n + 1) * part]

    def exchange_copy(phase, d):
        peer = peers[d]
        return angle_copy(
            phase, d,
            sends[phase].at[pl.ds(peer * capacity, capacity)],
            recvs[phase].at[pl.ds(g * capacity, capacity)],
        )

    own = pl.ds(g * capacity, capacity)
    fetches = [exchange_copy(0, d) for d in rising]
    for copy in fetches:
        copy.start()
    recv_a[own] = send_a[own]

    lax.fori_loop(1, rows_ref.shape[1] // CHUNK, step, 0)

    rims = [[], []]
    grads = []
    for channel in (1, 0):
        for side in range(2):
            rim_ref[0, channel, :, lanes[side]] = acc_ref[channel, side, HALO + band :].astype(half)
            rim_ref[1, channel, :, lanes[side]] = acc_ref[channel, side, :HALO].astype(half)
        for way in range(2):
            where = {"tile": below if way == 0 else upper}
            other = dict(where, half=1 - h)
            index = 6 + way * 5 + channel * 2
            pair_of = [
                near(index, rim_ref.at[way, channel, away, :], rim_here_ref.at[way, h, channel], other),
                near(index + 1, rim_ref.at[way, channel, here, :], rim_here_ref.at[way, h, channel], where),
            ]
            rims[way].append(pair_of)

            def send(copies=pair_of):
                for copy in copies:
                    copy.start()

            when_sent(way, send)
        for side in range(2):
            grad_ref[channel, :, lanes[side]] = acc_ref[channel, side, HALO : HALO + band]
        grads.append(
            near(4 + channel, grad_ref.at[channel, away, :], both_grad_ref.at[h, channel], {"half": 1 - h})
        )
        grads[-1].start()
    for way in range(2):
        where = {"tile": below if way == 0 else upper}
        rims[way].append([near(10 + way * 5, rim_ref.at[way, :, away, :], rim_away_ref.at[way], where)])
        when_sent(way, rims[way][-1][0].start)
    both_grad_ref[h] = grad_ref[:, here, :]
    tile_copy.wait_recv()
    beside = near(16, far_tile_ref.at[h, column], far_tile_ref.at[h, column], {"tile": t + 1 - 2 * column})
    beside.start()

    def projections(phase, arrivals):
        totals = [jnp.zeros((part, RB), jnp.float32)] * pairs
        for peer, copy in [(g, None)] + arrivals:
            if copy is not None:
                copy.wait_recv()
            for r in range(capacity):
                n = peer * capacity + r
                slot = slot_ref[n]
                term = lax.dot_general(
                    recvs[phase][n], weight_ref[slot], (((1,), (1,)), ((), ())),
                    preferred_element_type=jnp.float32,
                )
                for pair in range(pairs):
                    scale = jnp.where(lax.div(slot, per_block) == pair, used_ref[n], 0.0)
                    totals[pair] = totals[pair] + scale * term
        return totals

    def projected(phase, pair):
        total = jnp.zeros((part, RB), jnp.float32)
        for c in range(per_block):
            slot = pair * per_block + c
            picked = recvs[phase][place_ref[slot]]
            total = total + live_ref[slot] * lax.dot_general(
                picked, weight_ref[slot], (((1,), (1,)), ((), ())),
                preferred_element_type=jnp.float32,
            )
        return total

    for copy in fetches:
        copy.wait_recv()
    sinos = [projected(0, pair) for pair in range(pairs)]

    def received(stage):
        for way in range(2):
            def take(copies=rims[way][stage]):
                for copy in copies:
                    copy.wait_recv()

            when_received(way, take)

    def renewed(angle, channel):
        around = both_grad_ref[angle, channel] + rim_here_ref[0, angle, channel].astype(jnp.float32)
        around = around + rim_here_ref[1, angle, channel].astype(jnp.float32)
        return both_base_ref[angle, channel] - descent * around

    base_copy.wait_recv()
    mult_copy.wait_recv()
    grads[0].wait_recv()
    received(0)
    news = [renewed(angle, 1) for angle in range(angles)]
    for pair in range(pairs):
        angle, k = divmod(pair, NRB)
        rays = slice(k * RB, (k + 1) * RB)
        target = news[angle][:, rays] + both_mult_ref[angle, 1, :, rays] / penalty
        residual_ref[pair] = (sinos[pair] - target).astype(half)

    def spread(n):
        slot = slot_ref[n]
        term = dot(residual_ref[lax.div(slot, per_block)], weight_ref[slot])
        return (used_ref[n] * term).astype(half)

    for r in range(capacity):
        n = twin * capacity + r
        twin_send_ref[r] = residual_ref[lax.div(slot_ref[n], per_block)] * used_ref[n].astype(half)
    terms = [angle_copy(1, across, twin_send_ref, twin_recv_ref)]
    terms[0].start()
    for d in paired:
        if d == across:
            continue
        peer = peers[d]
        for r in range(capacity):
            send_b[peer * capacity + r] = spread(peer * capacity + r)
        terms.append(exchange_copy(1, d))
        terms[-1].start()
    for r in range(capacity):
        recv_b[g * capacity + r] = spread(g * capacity + r)

    beside.wait_recv()
    inside = near(17, far_tile_ref.at[h], far_tile_ref.at[h], {"half": 1 - h})
    inside.start()

    width = places * part
    per_tile = LANES // part
    tile_lane = lax.broadcasted_iota(jnp.int32, (1, LANES), 1)
    keys = []
    for first in range(0, places, per_tile):
        key = jnp.zeros((1, LANES), jnp.int32)
        for n in range(first, first + per_tile):
            q, r = divmod(n, capacity)
            key = jnp.where(tile_lane // part == n - first, all_ref[q, r : r + 1, :], key)
        keys.append(key * part + tile_lane % part)
    key = jnp.concatenate(keys, axis=1)
    merge_ref[...] = jnp.where(
        lax.broadcasted_iota(jnp.int32, (reach, width), 0) == key, 1.0, 0.0
    ).astype(half)

    grads[1].wait_recv()
    received(1)
    received(2)
    for angle in range(angles):
        new_mult_ref[angle, 0] = both_mult_ref[angle, 0] + penalty * (renewed(angle, 0) - 1.0)
    for channel in range(2):
        updated_ref[0, channel, here, :] = renewed(h, channel)
        far = grad_ref[channel, away, :] + rim_away_ref[0, channel].astype(jnp.float32)
        far = far + rim_away_ref[1, channel].astype(jnp.float32)
        updated_ref[0, channel, away, :] = base_ref[channel, away, :] - descent * far
    id_local.wait()
    inside.wait_recv()
    terms[0].wait_recv()
    far_tiles = [
        jnp.concatenate([far_tile_ref[k // 2, k % 2, r] for k in range(4)], axis=0)
        for r in range(capacity)
    ]
    for r in range(capacity):
        recv_b[twin * capacity + r] = dot(twin_recv_ref[r], far_tiles[r]).astype(half)
    for copy in terms[1:]:
        copy.wait_recv()
    total = dot(merge_ref[...], recv_b[...].reshape(width, PIX)).reshape(own_blocks, part, PIX)
    block = vol_ref[...]
    new_vol = block - volume_step * (total + damping * block)
    new_vol_ref[...] = new_vol
    vol_half_ref[...] = new_vol.astype(half)
    for r in range(capacity):
        part_send_ref[r] = lax.dot_general(
            vol_half_ref[all_smem[twin, r, 0]], far_tiles[r], (((1,), (1,)), ((), ())),
            preferred_element_type=jnp.float32,
        ).astype(half)
    renewals = [angle_copy(2, across, part_send_ref, part_recv_ref)]
    renewals[0].start()
    for d in paired:
        if d == across:
            continue
        peer = peers[d]
        for r in range(capacity):
            send_c[peer * capacity + r] = vol_half_ref[all_smem[peer, r, 0]]
        renewals.append(exchange_copy(2, d))
        renewals[-1].start()
    for r in range(capacity):
        recv_c[g * capacity + r] = vol_half_ref[all_smem[g, r, 0]]
    by_mask = dict(zip([d for d in paired if d != across], renewals[1:]))
    freshes = projections(2, [(peers[d], by_mask[d]) for d in rising if d != across])
    renewals[0].wait_recv()
    for pair in range(pairs):
        angle, k = divmod(pair, NRB)
        rays = slice(k * RB, (k + 1) * RB)
        fresh = freshes[pair]
        for r in range(capacity):
            n = twin * capacity + r
            mine = jnp.where(lax.div(slot_ref[n], per_block) == pair, used_ref[n], 0.0)
            fresh = fresh + mine * part_recv_ref[r].astype(jnp.float32)
        new_mult_ref[angle, 1, :, rays] = both_mult_ref[angle, 1, :, rays] + penalty * (
            news[angle][:, rays] - fresh
        )
    for copy in id_copies + fetches + terms + renewals + grads + [base_copy, mult_copy, tile_copy, beside, inside]:
        copy.wait_send()
    for way in range(2):
        def settle(copies=sum(rims[way], [halo[way]])):
            for copy in copies:
                copy.wait_send()

        when_sent(way, settle)


def admm_step(ray_blocks, counts, rows, cols, own, multiplier, prior, measured, field, mask, volume, weights):
    groups = lax.axis_size("angle")
    tiles = lax.axis_size("tile")
    slots = ray_blocks.size
    capacity = max(2, -(-slots // groups))
    places = groups * capacity
    left_f, right_f = dft_blocks(-1.0)
    left_b, right_b = dft_blocks(1.0)
    left_f, left_b = (split_table(m) for m in (left_f, left_b))
    tables = [left_f, jnp.asarray(right_f, jnp.bfloat16), left_b, jnp.asarray(right_b, jnp.bfloat16)]
    vmem = pl.BlockSpec(memory_space=pltpu.VMEM)
    band = own.shape[2]
    part = band // 2
    assert band == HALO and capacity <= ROWS and groups & (groups - 1) == 0 and tiles % 2 == 0
    ext_rows = band + 2 * HALO
    own_blocks = volume.shape[0]
    block = volume.shape[1:]
    weights = weights.reshape((slots,) + weights.shape[3:])
    f32 = jnp.float32
    half = jnp.bfloat16
    operands = [
        ray_blocks, counts, rows, cols, own, multiplier, prior, field, mask, *tables,
        measured, volume, weights,
    ]
    spaces = [pltpu.SMEM] * 4 + [pltpu.VMEM] * 12
    return pl.pallas_call(
        functools.partial(step_kernel, groups, tiles, capacity),
        out_shape=(
            jax.ShapeDtypeStruct(own.shape, f32),
            jax.ShapeDtypeStruct(volume.shape, f32),
            jax.ShapeDtypeStruct((2, 2, part, NW), f32),
        ),
        in_specs=[pl.BlockSpec(memory_space=pltpu.HBM)] * 16,
        out_specs=(vmem, vmem, vmem),
        scratch_shapes=[
            *[space(x.shape, x.dtype) for space, x in zip(spaces, operands)],
            pltpu.SMEM((groups, ROWS, LANES), jnp.int32),
            pltpu.SMEM((slots,), jnp.int32),
            pltpu.SMEM((slots,), jnp.int32),
            pltpu.SMEM((places,), jnp.int32),
            pltpu.SMEM((places,), f32),
            pltpu.SMEM((slots,), f32),
            pltpu.VMEM((groups, ROWS, LANES), jnp.int32),
            pltpu.VMEM((groups, ROWS, LANES), jnp.int32),
            pltpu.VMEM((2, HALO, NW), half),
            pltpu.VMEM((2, HALO, NW), half),
            pltpu.VMEM((2, HALO, NW), half),
            pltpu.VMEM((2, NW // PC, ext_rows, PC), f32),
            pltpu.VMEM((2, NW // PC, ext_rows, PC), f32),
            pltpu.VMEM((2, PR, PC), f32),
            pltpu.VMEM((CHUNK, 2, 2 * (ext_rows - PR) + PR, PC), f32),
            pltpu.VMEM((2, band, NW), f32),
            pltpu.VMEM((2, band, NW), f32),
            *[pltpu.VMEM((2, 2, part, NW), f32)] * 3,
            pltpu.VMEM((2, 2, HALO, NW), half),
            pltpu.VMEM((2, 2, 2, part, NW), half),
            pltpu.VMEM((2, 2, part, NW), half),
            pltpu.VMEM((own_blocks,) + block, half),
            pltpu.VMEM((own_blocks * part, places * part), half),
            pltpu.VMEM((slots // weights_per_block(ray_blocks), part, RB), half),
            pltpu.VMEM((capacity, RB // 4, PIX), half),
            pltpu.VMEM((2, 2, capacity, RB // 4, PIX), half),
            *[pltpu.VMEM((capacity, part, RB), half)] * 4,
            *[pltpu.VMEM((places,) + block, half)] * 6,
            pltpu.SemaphoreType.DMA((5, groups)),
            pltpu.SemaphoreType.DMA((5, groups)),
            pltpu.SemaphoreType.DMA((18,)),
            pltpu.SemaphoreType.DMA((18,)),
            pltpu.SemaphoreType.DMA((17,)),
        ],
        compiler_params=pltpu.CompilerParams(
            collective_id=1, has_side_effects=True, vmem_limit_bytes=32 * 1024 * 1024
        ),
    )(*[pltpu.with_memory_space_constraint(x, pltpu.HBM) for x in operands])


def weights_per_block(ray_blocks):
    return ray_blocks.shape[2]


def write_kernel(a_ref, b_ref, c_ref, a_out, b_out, c_out, sems):
    copies = [
        pltpu.make_async_copy(source, target, sems.at[i])
        for i, (source, target) in enumerate(((a_ref, a_out), (b_ref, b_out), (c_ref, c_out)))
    ]
    for copy in copies:
        copy.start()
    for copy in copies:
        copy.wait()


def write_out(values):
    return pl.pallas_call(
        write_kernel,
        out_shape=tuple(jax.ShapeDtypeStruct(v.shape, v.dtype) for v in values),
        in_specs=[pl.BlockSpec(memory_space=pltpu.VMEM)] * 3,
        out_specs=tuple([pl.BlockSpec(memory_space=pl.ANY)] * 3),
        scratch_shapes=[pltpu.SemaphoreType.DMA((3,))],
        compiler_params=pltpu.CompilerParams(vmem_limit_bytes=8 * 1024 * 1024),
    )(*values)


def shards(
    projection,
    multiplier,
    reprojection,
    intensity,
    row_start,
    column_start,
    probe_field,
    probe_mask,
    weights,
    ray_blocks,
    ray_counts,
    volume,
):
    return write_out(
        admm_step(
            ray_blocks, ray_counts, row_start, column_start, projection, multiplier, reprojection,
            intensity, probe_field, probe_mask, volume, weights,
        )
    )


def solution(mesh):
    return jax.shard_map(
        shards,
        mesh=mesh,
        in_specs=(
            P(("angle", "half"), None, "tile", None),
            P(("angle", "half"), None, "tile", None),
            P(("angle", "half"), "tile", None),
            P(("angle", "half"), "tile", None, None),
            P(("angle", "half"), "tile"),
            P(("angle", "half"), "tile"),
            P(),
            P(),
            P("angle", None, None, None, None),
            P("angle", None, None),
            P("angle", None),
            P("angle", ("tile", "half"), None),
        ),
        out_specs=(
            P(("angle", "half"), None, "tile", None),
            P("angle", ("tile", "half"), None),
            P("angle", None, ("tile", "half"), None),
        ),
        check_vma=False,
    )
```

```python
import functools

import jax
import jax.numpy as jnp
import numpy as np
from jax import lax
from jax.experimental import pallas as pl
from jax.experimental.pallas import tpu as pltpu
from jax.sharding import PartitionSpec as P

PR = 64
PC = 128
NW = 256
PIX = 512
RB = 128
CMAX = 4
HALO = 32
NRB = 2


penalty = 0.5
descent = 0.25
volume_step = 1.0
damping = 0.1


def dft_blocks(sign):
    def table(length):
        counter = np.arange(length)
        phase = (counter[:, None] * counter[None, :] % length) * (2.0 * np.pi / length)
        return np.cos(phase) / np.sqrt(length), sign * np.sin(phase) / np.sqrt(length)

    row_cos, row_sin = table(PR)
    col_cos, col_sin = table(PC)
    left = np.block([[row_cos, -row_sin], [row_sin, row_cos]])
    right = np.block([[col_cos, col_sin], [-col_sin, col_cos]])
    return left.astype(np.float32), right.astype(np.float32)


def split_table(matrix):
    coarse = matrix.astype(jnp.bfloat16)
    rest = (matrix - coarse.astype(np.float32)).astype(jnp.bfloat16)
    return jnp.asarray(np.concatenate([coarse, rest], axis=1))


MESH = pl.DeviceIdType.MESH
CHUNK = 16
ROWS = 8
LANES = 128


def orders(groups):
    rising = list(range(1, groups))
    return rising, [groups // 2] + [d for d in reversed(rising) if 2 * d != groups]


def flipped(index, mask, count):
    out = jnp.int32(0)
    bit = 1
    while bit < count:
        out = out + lax.rem(lax.div(index, bit) + mask // bit, 2) * bit
        bit *= 2
    return out


def step_kernel(
    groups, tiles, capacity,
    mine_hbm, counts_hbm, rows_hbm, cols_hbm, proj_hbm, mult_hbm, prior_hbm, field_hbm, mask_hbm,
    left_f_hbm, right_f_hbm, left_b_hbm, right_b_hbm, measured_hbm, vol_hbm, weight_hbm,
    updated_ref, new_vol_ref, new_mult_ref,
    mine_ref, counts_ref, rows_ref, cols_ref, proj_ref, mult_ref, prior_ref, field_ref, mask_ref,
    left_f_ref, right_f_ref, left_b_ref, right_b_ref, measured_ref, vol_ref, weight_ref,
    all_smem, place_ref, inside_ref, slot_ref, used_ref, live_ref,
    ids_ref, all_ref, edge_ref, before_ref, after_ref,
    ext_ref, acc_ref, wave_ref, stage_ref,
    base_ref, grad_ref, both_base_ref, both_mult_ref, both_grad_ref,
    rim_ref, rim_here_ref, rim_away_ref,
    vol_half_ref, merge_ref, residual_ref,
    tile_ref, far_tile_ref, twin_send_ref, twin_recv_ref, part_send_ref, part_recv_ref,
    send_a, send_b, send_c, recv_a, recv_b, recv_c,
    send_sem, recv_sem, near_send, near_recv, local_sem,
):
    g = lax.axis_index("angle")
    t = lax.axis_index("tile")
    h = lax.axis_index("half")
    band = proj_ref.shape[2]
    part = band // 2
    places = groups * capacity
    own_blocks = vol_ref.shape[0]
    angles, blocks, per_block = mine_ref.shape
    slots = angles * blocks * per_block
    pairs = slots // per_block
    has_up = t > 0
    has_down = t < tiles - 1
    half = jnp.bfloat16
    sends = (send_a, send_b, send_c)
    recvs = (recv_a, recv_b, recv_c)
    lanes = [slice(0, PC), slice(PC, NW)]
    rising, paired = orders(groups)
    peers = {m: flipped(g, m, groups) for m in rising}
    for m in [m for m in rising[1:] if m // 2 != groups // 4]:
        peers[m] = peers[m] + h * (1 - 2 * lax.rem(peers[m], 2))
    across = groups // 2
    twin = peers[across]
    column = lax.rem(t, 2)
    quarter = RB // 4

    def where_of(slot):
        pair, c = divmod(slot, per_block)
        angle, block = divmod(pair, blocks)
        return angle, block, c

    barrier = pltpu.get_barrier_semaphore()

    def greet(where):
        pl.semaphore_signal(barrier, inc=1, device_id=where, device_id_type=MESH)

    for d in rising:
        greet({"angle": peers[d]})
    greet({"half": 1 - h})

    @pl.when(has_up)
    def _():
        greet({"tile": t - 1})
        greet({"tile": t - 1, "half": 1 - h})

    @pl.when(has_down)
    def _():
        greet({"tile": t + 1})
        greet({"tile": t + 1, "half": 1 - h})

    sources = (
        mine_hbm, counts_hbm, rows_hbm, cols_hbm, proj_hbm, mult_hbm, prior_hbm, field_hbm, mask_hbm,
        left_f_hbm, right_f_hbm, left_b_hbm, right_b_hbm, measured_hbm, vol_hbm, weight_hbm,
    )
    targets = (
        mine_ref, counts_ref, rows_ref, cols_ref, proj_ref, mult_ref, prior_ref, field_ref, mask_ref,
        left_f_ref, right_f_ref, left_b_ref, right_b_ref, measured_ref, vol_ref, weight_ref,
    )
    loads = [
        pltpu.make_async_copy(source, target, local_sem.at[i])
        for i, (source, target) in enumerate(zip(sources, targets))
    ]
    for load in loads:
        load.start()

    @pl.when(jnp.logical_not(has_up))
    def _():
        before_ref[...] = jnp.zeros_like(before_ref)
        rim_here_ref[0] = jnp.zeros(rim_here_ref.shape[1:], half)
        rim_away_ref[0] = jnp.zeros(rim_away_ref.shape[1:], half)

    @pl.when(jnp.logical_not(has_down))
    def _():
        after_ref[...] = jnp.zeros_like(after_ref)
        rim_here_ref[1] = jnp.zeros(rim_here_ref.shape[1:], half)
        rim_away_ref[1] = jnp.zeros(rim_away_ref.shape[1:], half)

    acc_ref[...] = jnp.zeros_like(acc_ref)
    stage_ref[...] = jnp.zeros_like(stage_ref)
    ids_ref[...] = jnp.zeros_like(ids_ref)

    for load in loads[:2]:
        load.wait()
    blocks_of = [mine_ref[where_of(s)] for s in range(slots)]
    owners = [lax.div(b, own_blocks) for b in blocks_of]
    for s in range(slots):
        rank = jnp.int32(0)
        for earlier in range(s):
            rank = rank + jnp.where(owners[earlier] == owners[s], 1, 0)
        place_ref[s] = owners[s] * capacity + rank
        inside_ref[s] = lax.rem(blocks_of[s], own_blocks)
        angle, block, c = where_of(s)
        live_ref[s] = jnp.where(c < counts_ref[angle, block], 1.0, 0.0)

    def slot_of(n, carry):
        slot = jnp.int32(0)
        used = jnp.float32(0.0)
        for s in range(slots):
            hit = place_ref[s] == n
            slot = jnp.where(hit, s, slot)
            used = jnp.where(hit, live_ref[s], used)
        slot_ref[n] = slot
        used_ref[n] = used
        return carry

    lax.fori_loop(0, places, slot_of, 0)
    for n in range(places):
        q, r = divmod(n, capacity)
        ids_ref[q, r : r + 1, :] = jnp.full((1, LANES), inside_ref[slot_ref[n]], jnp.int32)

    away = pl.ds(pl.multiple_of((1 - h) * part, part), part)
    here = pl.ds(pl.multiple_of(h * part, part), part)
    for load in loads[4:9]:
        load.wait()
    edge_ref[...] = proj_ref[0].astype(half)
    for channel in range(2):
        old = proj_ref[0, channel]
        held = 1.0 if channel == 0 else prior_ref[0]
        base_ref[channel] = old - descent * (penalty * (old - held) + mult_ref[0, channel])
    for side in range(2):
        ext_ref[:, side, HALO : HALO + band] = proj_ref[0, :, :, lanes[side]]
    mask = mask_ref[...].astype(jnp.float32)
    wave_ref[0] = field_ref[0] * mask
    wave_ref[1] = field_ref[1] * mask
    both_base_ref[h] = base_ref[:, here, :]
    both_mult_ref[h] = mult_ref[0, :, here, :]
    pl.semaphore_wait(
        barrier, groups + 2 * has_up.astype(jnp.int32) + 2 * has_down.astype(jnp.int32)
    )

    def angle_copy(phase, d, source, target):
        return pltpu.make_async_remote_copy(
            src_ref=source,
            dst_ref=target,
            send_sem=send_sem.at[phase, d],
            recv_sem=recv_sem.at[phase, d],
            device_id={"angle": peers[d]},
            device_id_type=MESH,
        )

    def near(index, source, target, where):
        return pltpu.make_async_remote_copy(
            src_ref=source,
            dst_ref=target,
            send_sem=near_send.at[index],
            recv_sem=near_recv.at[index],
            device_id=where,
            device_id_type=MESH,
        )

    below = jnp.minimum(t + 1, tiles - 1)
    upper = jnp.maximum(t - 1, 0)

    def when_sent(way, act):
        pl.when(has_down if way == 0 else has_up)(act)

    def when_received(way, act):
        pl.when(has_up if way == 0 else has_down)(act)

    id_copies = [
        angle_copy(3, d, ids_ref.at[peers[d]], all_ref.at[g]) for d in rising
    ]
    for copy in id_copies:
        copy.start()
    halo = [
        near(0, edge_ref, before_ref, {"tile": below}),
        near(1, edge_ref, after_ref, {"tile": upper}),
    ]
    for way in range(2):
        when_sent(way, halo[way].start)
    base_copy = near(2, base_ref.at[:, away, :], both_base_ref.at[h], {"half": 1 - h})
    mult_copy = near(3, mult_ref.at[0, :, away, :], both_mult_ref.at[h], {"half": 1 - h})
    base_copy.start()
    mult_copy.start()
    loads[14].wait()
    vol_half_ref[...] = vol_ref[...].astype(half)
    loads[15].wait()
    first_ray = pl.multiple_of((2 * h + column) * quarter, quarter)
    for r in range(capacity):
        tile_ref[r] = weight_ref[slot_ref[twin * capacity + r], pl.ds(first_ray, quarter), :]

    tile_copy = angle_copy(4, across, tile_ref, far_tile_ref.at[h, column])
    tile_copy.start()
    all_ref[g] = ids_ref[g]
    for load in loads[2:4] + loads[9:14]:
        load.wait()
    for way in range(2):
        when_received(way, halo[way].wait_recv)
    for side in range(2):
        ext_ref[:, side, :HALO] = before_ref[:, :, lanes[side]].astype(jnp.float32)
        ext_ref[:, side, HALO + band :] = after_ref[:, :, lanes[side]].astype(jnp.float32)

    lane = lax.broadcasted_iota(jnp.int32, (PR, PC), 1)
    ext_rows = band + 2 * HALO
    wide_lane = lax.broadcasted_iota(jnp.int32, (ext_rows, PC), 1)

    def dot(a, b):
        return jnp.dot(a, b, preferred_element_type=jnp.float32)

    def step(chunk, carry):
        waves = []
        spots = []
        for j in range(CHUNK):
            p = chunk * CHUNK + j
            row = rows_ref[0, p] + HALO
            col = cols_ref[0, p]
            spots.append((row, col))
            back_shift = lax.rem(NW - col, PC)

            def window(channel):
                near = pltpu.roll(ext_ref[channel, 0, pl.ds(row, PR), :], back_shift, 1)
                next_ = pltpu.roll(ext_ref[channel, 1, pl.ds(row, PR), :], back_shift, 1)
                return jnp.where(lane + col < PC, near, next_)

            o_re = window(0)
            o_im = window(1)
            p_re, p_im = wave_ref[0], wave_ref[1]
            waves.append(
                jnp.concatenate([p_re * o_re - p_im * o_im, p_re * o_im + p_im * o_re], axis=0)
            )
        wide = jnp.concatenate(waves, axis=1).astype(half)
        first = dot(left_f_ref[...], jnp.concatenate([wide, wide], axis=0)).astype(half)
        tall = jnp.concatenate(
            [
                jnp.concatenate(
                    [first[:PR, j * PC : (j + 1) * PC], first[PR:, j * PC : (j + 1) * PC]], axis=1
                )
                for j in range(CHUNK)
            ],
            axis=0,
        )
        far = dot(tall, right_f_ref[...])
        f_re, f_im = far[:, :PC], far[:, PC:]
        measured = measured_ref[0, pl.ds(chunk * CHUNK, CHUNK)].astype(jnp.float32)
        measured = measured.reshape(CHUNK * PR, PC)
        factor = 1.0 - jnp.sqrt(measured) * lax.rsqrt(f_re * f_re + f_im * f_im + 1.0)
        scaled = jnp.concatenate([f_re * factor, f_im * factor], axis=1).astype(half)
        second = dot(scaled, right_b_ref[...]).astype(half)
        wide = jnp.concatenate(
            [
                jnp.concatenate(
                    [second[j * PR : (j + 1) * PR, :PC], second[j * PR : (j + 1) * PR, PC:]], axis=0
                )
                for j in range(CHUNK)
            ],
            axis=1,
        )
        back = dot(left_b_ref[...], jnp.concatenate([wide, wide], axis=0))
        above = ext_rows - PR
        for j in range(CHUNK):
            shift = lax.rem(spots[j][1], PC)
            b_re = back[:PR, j * PC : (j + 1) * PC]
            b_im = back[PR:, j * PC : (j + 1) * PC]
            p_re, p_im = wave_ref[0], wave_ref[1]
            stage_ref[j, 0, above : above + PR] = pltpu.roll(p_re * b_re + p_im * b_im, shift, 1)
            stage_ref[j, 1, above : above + PR] = pltpu.roll(p_re * b_im - p_im * b_re, shift, 1)
        for channel in range(2):
            first_half = acc_ref[channel, 0]
            next_half = acc_ref[channel, 1]
            for j in range(CHUNK):
                row, col = spots[j]
                values = stage_ref[j, channel, pl.ds(above - row, ext_rows), :]
                first_half = first_half + jnp.where(wide_lane >= col, values, 0.0)
                next_half = next_half + jnp.where(wide_lane >= col, 0.0, values)
            acc_ref[channel, 0] = first_half
            acc_ref[channel, 1] = next_half
        return carry

    lax.fori_loop(0, 1, step, 0)

    for copy in id_copies:
        copy.wait_recv()
    id_local = pltpu.make_async_copy(all_ref, all_smem, local_sem.at[len(loads)])
    id_local.start()
    reach = own_blocks * part
    skew = lax.broadcasted_iota(jnp.int32, (part, reach), 1) - lax.broadcasted_iota(
        jnp.int32, (part, reach), 0
    )
    picks = []
    for n in range(places):
        q, r = divmod(n, capacity)
        want = jnp.concatenate([all_ref[q, r : r + 1, :]] * (reach // LANES), axis=1)
        picks.append(jnp.where(skew == want * part, 1.0, 0.0).astype(half))
    gathered = dot(jnp.concatenate(picks, axis=0), vol_half_ref[...].reshape(reach, PIX)).astype(half)
    for n in range(places):
        send_a[n] = gathered[n * part : (n + 1) * part]

    def exchange_copy(phase, d):
        peer = peers[d]
        return angle_copy(
            phase, d,
            sends[phase].at[pl.ds(peer * capacity, capacity)],
            recvs[phase].at[pl.ds(g * capacity, capacity)],
        )

    own = pl.ds(g * capacity, capacity)
    fetches = [exchange_copy(0, d) for d in rising]
    for copy in fetches:
        copy.start()
    recv_a[own] = send_a[own]

    lax.fori_loop(1, rows_ref.shape[1] // CHUNK, step, 0)

    rims = [[], []]
    grads = []
    for channel in (1, 0):
        for side in range(2):
            rim_ref[0, channel, :, lanes[side]] = acc_ref[channel, side, HALO + band :].astype(half)
            rim_ref[1, channel, :, lanes[side]] = acc_ref[channel, side, :HALO].astype(half)
        for way in range(2):
            where = {"tile": below if way == 0 else upper}
            other = dict(where, half=1 - h)
            index = 6 + way * 5 + channel * 2
            pair_of = [
                near(index, rim_ref.at[way, channel, away, :], rim_here_ref.at[way, h, channel], other),
                near(index + 1, rim_ref.at[way, channel, here, :], rim_here_ref.at[way, h, channel], where),
            ]
            rims[way].append(pair_of)

            def send(copies=pair_of):
                for copy in copies:
                    copy.start()

            when_sent(way, send)
        for side in range(2):
            grad_ref[channel, :, lanes[side]] = acc_ref[channel, side, HALO : HALO + band]
        grads.append(
            near(4 + channel, grad_ref.at[channel, away, :], both_grad_ref.at[h, channel], {"half": 1 - h})
        )
        grads[-1].start()
    for way in range(2):
        where = {"tile": below if way == 0 else upper}
        rims[way].append([near(10 + way * 5, rim_ref.at[way, :, away, :], rim_away_ref.at[way], where)])
        when_sent(way, rims[way][-1][0].start)
    both_grad_ref[h] = grad_ref[:, here, :]
    tile_copy.wait_recv()
    beside = near(16, far_tile_ref.at[h, column], far_tile_ref.at[h, column], {"tile": t + 1 - 2 * column})
    beside.start()

    def projections(phase, arrivals):
        totals = [jnp.zeros((part, RB), jnp.float32)] * pairs
        for peer, copy in [(g, None)] + arrivals:
            if copy is not None:
                copy.wait_recv()
            for r in range(capacity):
                n = peer * capacity + r
                slot = slot_ref[n]
                term = lax.dot_general(
                    recvs[phase][n], weight_ref[slot], (((1,), (1,)), ((), ())),
                    preferred_element_type=jnp.float32,
                )
                for pair in range(pairs):
                    scale = jnp.where(lax.div(slot, per_block) == pair, used_ref[n], 0.0)
                    totals[pair] = totals[pair] + scale * term
        return totals

    def projected(phase, pair):
        total = jnp.zeros((part, RB), jnp.float32)
        for c in range(per_block):
            slot = pair * per_block + c
            picked = recvs[phase][place_ref[slot]]
            total = total + live_ref[slot] * lax.dot_general(
                picked, weight_ref[slot], (((1,), (1,)), ((), ())),
                preferred_element_type=jnp.float32,
            )
        return total

    for copy in fetches:
        copy.wait_recv()
    sinos = [projected(0, pair) for pair in range(pairs)]

    def received(stage):
        for way in range(2):
            def take(copies=rims[way][stage]):
                for copy in copies:
                    copy.wait_recv()

            when_received(way, take)

    def renewed(angle, channel):
        around = both_grad_ref[angle, channel] + rim_here_ref[0, angle, channel].astype(jnp.float32)
        around = around + rim_here_ref[1, angle, channel].astype(jnp.float32)
        return both_base_ref[angle, channel] - descent * around

    base_copy.wait_recv()
    mult_copy.wait_recv()
    grads[0].wait_recv()
    received(0)
    news = [renewed(angle, 1) for angle in range(angles)]
    for pair in range(pairs):
        angle, k = divmod(pair, NRB)
        rays = slice(k * RB, (k + 1) * RB)
        target = news[angle][:, rays] + both_mult_ref[angle, 1, :, rays] / penalty
        residual_ref[pair] = (sinos[pair] - target).astype(half)

    def spread(n):
        slot = slot_ref[n]
        term = dot(residual_ref[lax.div(slot, per_block)], weight_ref[slot])
        return (used_ref[n] * term).astype(half)

    for r in range(capacity):
        n = twin * capacity + r
        twin_send_ref[r] = residual_ref[lax.div(slot_ref[n], per_block)] * used_ref[n].astype(half)
    terms = [angle_copy(1, across, twin_send_ref, twin_recv_ref)]
    terms[0].start()
    for d in paired:
        if d == across:
            continue
        peer = peers[d]
        for r in range(capacity):
            send_b[peer * capacity + r] = spread(peer * capacity + r)
        terms.append(exchange_copy(1, d))
        terms[-1].start()
    for r in range(capacity):
        recv_b[g * capacity + r] = spread(g * capacity + r)

    beside.wait_recv()
    inside = near(17, far_tile_ref.at[h], far_tile_ref.at[h], {"half": 1 - h})
    inside.start()

    width = places * part
    per_tile = LANES // part
    tile_lane = lax.broadcasted_iota(jnp.int32, (1, LANES), 1)
    keys = []
    for first in range(0, places, per_tile):
        key = jnp.zeros((1, LANES), jnp.int32)
        for n in range(first, first + per_tile):
            q, r = divmod(n, capacity)
            key = jnp.where(tile_lane // part == n - first, all_ref[q, r : r + 1, :], key)
        keys.append(key * part + tile_lane % part)
    key = jnp.concatenate(keys, axis=1)
    merge_ref[...] = jnp.where(
        lax.broadcasted_iota(jnp.int32, (reach, width), 0) == key, 1.0, 0.0
    ).astype(half)

    grads[1].wait_recv()
    received(1)
    received(2)
    for angle in range(angles):
        new_mult_ref[angle, 0] = both_mult_ref[angle, 0] + penalty * (renewed(angle, 0) - 1.0)
    for channel in range(2):
        updated_ref[0, channel, here, :] = renewed(h, channel)
        far = grad_ref[channel, away, :] + rim_away_ref[0, channel].astype(jnp.float32)
        far = far + rim_away_ref[1, channel].astype(jnp.float32)
        updated_ref[0, channel, away, :] = base_ref[channel, away, :] - descent * far
    id_local.wait()
    inside.wait_recv()
    terms[0].wait_recv()
    far_tiles = [
        jnp.concatenate([far_tile_ref[k // 2, k % 2, r] for k in range(4)], axis=0)
        for r in range(capacity)
    ]
    for r in range(capacity):
        recv_b[twin * capacity + r] = dot(twin_recv_ref[r], far_tiles[r]).astype(half)
    for copy in terms[1:]:
        copy.wait_recv()
    total = dot(merge_ref[...], recv_b[...].reshape(width, PIX)).reshape(own_blocks, part, PIX)
    block = vol_ref[...]
    new_vol = block - volume_step * (total + damping * block)
    new_vol_ref[...] = new_vol
    vol_half_ref[...] = new_vol.astype(half)
    for r in range(capacity):
        part_send_ref[r] = lax.dot_general(
            vol_half_ref[all_smem[twin, r, 0]], far_tiles[r], (((1,), (1,)), ((), ())),
            preferred_element_type=jnp.float32,
        ).astype(half)
    renewals = [angle_copy(2, across, part_send_ref, part_recv_ref)]
    renewals[0].start()
    for d in paired:
        if d == across:
            continue
        peer = peers[d]
        for r in range(capacity):
            send_c[peer * capacity + r] = vol_half_ref[all_smem[peer, r, 0]]
        renewals.append(exchange_copy(2, d))
        renewals[-1].start()
    for r in range(capacity):
        recv_c[g * capacity + r] = vol_half_ref[all_smem[g, r, 0]]
    by_mask = dict(zip([d for d in paired if d != across], renewals[1:]))
    freshes = projections(2, [(peers[d], by_mask[d]) for d in rising if d != across])
    renewals[0].wait_recv()
    for pair in range(pairs):
        angle, k = divmod(pair, NRB)
        rays = slice(k * RB, (k + 1) * RB)
        fresh = freshes[pair]
        for r in range(capacity):
            n = twin * capacity + r
            mine = jnp.where(lax.div(slot_ref[n], per_block) == pair, used_ref[n], 0.0)
            fresh = fresh + mine * part_recv_ref[r].astype(jnp.float32)
        new_mult_ref[angle, 1, :, rays] = both_mult_ref[angle, 1, :, rays] + penalty * (
            news[angle][:, rays] - fresh
        )
    for copy in id_copies + fetches + terms + renewals + grads + [base_copy, mult_copy, tile_copy, beside, inside]:
        copy.wait_send()
    for way in range(2):
        def settle(copies=sum(rims[way], [halo[way]])):
            for copy in copies:
                copy.wait_send()

        when_sent(way, settle)


def admm_step(ray_blocks, counts, rows, cols, own, multiplier, prior, measured, field, mask, volume, weights):
    groups = lax.axis_size("angle")
    tiles = lax.axis_size("tile")
    slots = ray_blocks.size
    capacity = max(2, -(-slots // groups))
    places = groups * capacity
    left_f, right_f = dft_blocks(-1.0)
    left_b, right_b = dft_blocks(1.0)
    left_f, left_b = (split_table(m) for m in (left_f, left_b))
    tables = [left_f, jnp.asarray(right_f, jnp.bfloat16), left_b, jnp.asarray(right_b, jnp.bfloat16)]
    vmem = pl.BlockSpec(memory_space=pltpu.VMEM)
    band = own.shape[2]
    part = band // 2
    assert band == HALO and capacity <= ROWS and groups & (groups - 1) == 0 and tiles % 2 == 0
    ext_rows = band + 2 * HALO
    own_blocks = volume.shape[0]
    block = volume.shape[1:]
    weights = weights.reshape((slots,) + weights.shape[3:])
    f32 = jnp.float32
    half = jnp.bfloat16
    operands = [
        ray_blocks, counts, rows, cols, own, multiplier, prior, field, mask, *tables,
        measured, volume, weights,
    ]
    spaces = [pltpu.SMEM] * 4 + [pltpu.VMEM] * 12
    return pl.pallas_call(
        functools.partial(step_kernel, groups, tiles, capacity),
        out_shape=(
            jax.ShapeDtypeStruct(own.shape, f32),
            jax.ShapeDtypeStruct(volume.shape, f32),
            jax.ShapeDtypeStruct((2, 2, part, NW), f32),
        ),
        in_specs=[pl.BlockSpec(memory_space=pltpu.HBM)] * 16,
        out_specs=(vmem, vmem, vmem),
        scratch_shapes=[
            *[space(x.shape, x.dtype) for space, x in zip(spaces, operands)],
            pltpu.SMEM((groups, ROWS, LANES), jnp.int32),
            pltpu.SMEM((slots,), jnp.int32),
            pltpu.SMEM((slots,), jnp.int32),
            pltpu.SMEM((places,), jnp.int32),
            pltpu.SMEM((places,), f32),
            pltpu.SMEM((slots,), f32),
            pltpu.VMEM((groups, ROWS, LANES), jnp.int32),
            pltpu.VMEM((groups, ROWS, LANES), jnp.int32),
            pltpu.VMEM((2, HALO, NW), half),
            pltpu.VMEM((2, HALO, NW), half),
            pltpu.VMEM((2, HALO, NW), half),
            pltpu.VMEM((2, NW // PC, ext_rows, PC), f32),
            pltpu.VMEM((2, NW // PC, ext_rows, PC), f32),
            pltpu.VMEM((2, PR, PC), f32),
            pltpu.VMEM((CHUNK, 2, 2 * (ext_rows - PR) + PR, PC), f32),
            pltpu.VMEM((2, band, NW), f32),
            pltpu.VMEM((2, band, NW), f32),
            *[pltpu.VMEM((2, 2, part, NW), f32)] * 3,
            pltpu.VMEM((2, 2, HALO, NW), half),
            pltpu.VMEM((2, 2, 2, part, NW), half),
            pltpu.VMEM((2, 2, part, NW), half),
            pltpu.VMEM((own_blocks,) + block, half),
            pltpu.VMEM((own_blocks * part, places * part), half),
            pltpu.VMEM((slots // weights_per_block(ray_blocks), part, RB), half),
            pltpu.VMEM((capacity, RB // 4, PIX), half),
            pltpu.VMEM((2, 2, capacity, RB // 4, PIX), half),
            *[pltpu.VMEM((capacity, part, RB), half)] * 4,
            *[pltpu.VMEM((places,) + block, half)] * 6,
            pltpu.SemaphoreType.DMA((5, groups)),
            pltpu.SemaphoreType.DMA((5, groups)),
            pltpu.SemaphoreType.DMA((18,)),
            pltpu.SemaphoreType.DMA((18,)),
            pltpu.SemaphoreType.DMA((17,)),
        ],
        compiler_params=pltpu.CompilerParams(
            collective_id=1, has_side_effects=True, vmem_limit_bytes=32 * 1024 * 1024
        ),
    )(*[pltpu.with_memory_space_constraint(x, pltpu.HBM) for x in operands])


def weights_per_block(ray_blocks):
    return ray_blocks.shape[2]


def write_kernel(a_ref, b_ref, c_ref, a_out, b_out, c_out, sems):
    copies = [
        pltpu.make_async_copy(source, target, sems.at[i])
        for i, (source, target) in enumerate(((a_ref, a_out), (b_ref, b_out), (c_ref, c_out)))
    ]
    for copy in copies:
        copy.start()
    for copy in copies:
        copy.wait()


def write_out(values):
    return pl.pallas_call(
        write_kernel,
        out_shape=tuple(jax.ShapeDtypeStruct(v.shape, v.dtype) for v in values),
        in_specs=[pl.BlockSpec(memory_space=pltpu.VMEM)] * 3,
        out_specs=tuple([pl.BlockSpec(memory_space=pl.ANY)] * 3),
        scratch_shapes=[pltpu.SemaphoreType.DMA((3,))],
        compiler_params=pltpu.CompilerParams(vmem_limit_bytes=8 * 1024 * 1024),
    )(*values)


def shards(
    projection,
    multiplier,
    reprojection,
    intensity,
    row_start,
    column_start,
    probe_field,
    probe_mask,
    weights,
    ray_blocks,
    ray_counts,
    volume,
):
    return write_out(
        admm_step(
            ray_blocks, ray_counts, row_start, column_start, projection, multiplier, reprojection,
            intensity, probe_field, probe_mask, volume, weights,
        )
    )


def solution(mesh):
    return jax.shard_map(
        shards,
        mesh=mesh,
        in_specs=(
            P(("angle", "half"), None, "tile", None),
            P(("angle", "half"), None, "tile", None),
            P(("angle", "half"), "tile", None),
            P(("angle", "half"), "tile", None, None),
            P(("angle", "half"), "tile"),
            P(("angle", "half"), "tile"),
            P(),
            P(),
            P("angle", None, None, None, None),
            P("angle", None, None),
            P("angle", None),
            P("angle", ("tile", "half"), None),
        ),
        out_specs=(
            P(("angle", "half"), None, "tile", None),
            P("angle", ("tile", "half"), None),
            P("angle", None, ("tile", "half"), None),
        ),
        check_vma=False,
    )
```
